512 devices in a mesh: qrow: 16 (over z_lo, y), kcol: 32 (over z_hi, x, core).
Axes of the slice: x: 4, y: 8, z: 8 (z_hi: 4, z_lo: 2; z = z_hi * 2 + z_lo), core: 2. Of those that a mesh axis runs over, the one named last changes fastest.
Arguments:
- queries: bfloat16 [32768, 512], P(('qrow', 'kcol')), may hold values from -6 to 6
- keys: bfloat16 [32768, 128], P(('kcol', 'qrow')), may hold values from -6 to 6
- values: bfloat16 [32768, 128], P(('kcol', 'qrow')), may hold values from -6 to 6
- block_mask: int32 [256, 256], replicated, may hold values from 0 to 1, as said below
Outputs:
- attended: float32 [32768, 512], P(('qrow', 'kcol'))
The draws below stay inside these ranges and needn't reach their ends.
Inputs may be any that keep to these rules, and one draw needn't show every extreme that they name: block_mask[a, b] is 1 only where b <= a, and always where 0 <= a - b < 3.
All inputs are finite; a program needn't handle non-finite values.
Results may differ from the reference program's by a relative error of at most 0.0022.
Values may be sent and summed in bfloat16 or wider, within the bound.
No kernel may reach another device: no remote copies, remote signals or barrier semaphores. Data moves between devices by JAX's collectives and lax.ppermute only.
A program may use at most 64 MiB of HBM per device.

```python
import math
import jax
import jax.numpy as jnp
from jax import lax

H = 4
DH = 128
BLOCK = 128
QBT = 16
S = 32768
NB = 256


def draw_queries(key, part):
    base_rows = jnp.clip(jax.random.normal(jax.random.fold_in(key, 11), (S, H * DH)), -6.0, 6.0)
    return base_rows.astype(jnp.bfloat16)


def draw_keys(key, part):
    base_rows = jnp.clip(jax.random.normal(jax.random.fold_in(key, 12), (S, DH)), -6.0, 6.0)
    return base_rows.astype(jnp.bfloat16)


def draw_block_mask(key, part):
    row_ids = jnp.arange(NB, dtype=jnp.int32)[:, None]
    col_ids = jnp.arange(NB, dtype=jnp.int32)[None, :]
    distance = row_ids - col_ids
    picks = jax.random.randint(jax.random.fold_in(key, 14), (NB, NB), 0, 100)
    semantic = (col_ids % 2 == 0) & (picks < 55)
    listed = (distance >= 0) & ((distance < 3) | semantic | (picks < 15))
    return listed.astype(jnp.int32)


def level_of(key, extent, cuts, smallest, top_value):
    gain = 1.0
    for axis_at, blocks in cuts:
        draws = jax.random.uniform(jax.random.fold_in(jax.random.fold_in(key, 6), axis_at), (blocks,), jnp.float32, smallest / len(cuts), top_value / len(cuts))
        gain = gain * jnp.repeat(jnp.exp(draws), extent[axis_at] // blocks).reshape((-1,) + (1,) * (len(extent) - 1 - axis_at))
    return gain


def noise(own_key, shape, scale, most, split=(), kind=jnp.bfloat16):
    level = level_of(own_key, shape, split, -0.22, 0.18) if split else 1.0
    entries = jax.random.normal(own_key, shape, jnp.float32) * scale * level
    return jnp.minimum(jnp.maximum(entries, -most), most).astype(kind)


def setup_inputs(seed: int = 0) -> dict:
    key_list = jax.random.split(jax.random.key(seed), 5)
    return {
        "queries": draw_queries(jax.random.fold_in(key_list[4], 71), 0),
        "keys": draw_keys(jax.random.fold_in(key_list[4], 71), 0),
        "values": noise(key_list[2], (S, DH), 1.0, 6.0, ((0, 512),)),
        "block_mask": draw_block_mask(jax.random.fold_in(key_list[4], 71), 0),
    }


NEG_FILL = -1e+30

def reference(queries, keys, values, block_mask):
    inv_root = 1.0 / math.sqrt(DH)
    query_wide = queries.astype(jnp.float32)
    key_wide = keys.astype(jnp.float32)
    value_wide = values.astype(jnp.float32)
    group_rows = QBT * BLOCK
    pieces = []
    for group in range(S // group_rows):
        end_tok = (group + 1) * group_rows
        end_blk = end_tok // BLOCK
        key_part = key_wide[:end_tok]
        value_part = value_wide[:end_tok].reshape(end_blk, BLOCK, DH)
        key_pos = jnp.arange(end_tok, dtype=jnp.int32)

        def one_block(block_index, key_part=key_part, value_part=value_part, key_pos=key_pos, end_blk=end_blk):
            first_row = block_index * BLOCK
            query_heads = lax.dynamic_slice_in_dim(query_wide, first_row, BLOCK, 0).reshape(BLOCK, H, DH)
            scores = jnp.einsum('rhd,kd->hrk', query_heads, key_part, precision=lax.Precision.HIGHEST) * inv_root
            mask_row = lax.dynamic_index_in_dim(block_mask, block_index, 0, keepdims=False)[:end_blk]
            listed = jnp.repeat(mask_row, BLOCK) == 1
            query_pos = first_row + jnp.arange(BLOCK, dtype=jnp.int32)
            permitted = listed[None, :] & (key_pos[None, :] <= query_pos[:, None])
            permitted = permitted.reshape(BLOCK, end_blk, BLOCK)
            scores = scores.reshape(H, BLOCK, end_blk, BLOCK)
            scores = jnp.where(permitted[None], scores, NEG_FILL)
            block_top = lax.optimization_barrier(jnp.max(scores, axis=3))
            weights = jnp.where(permitted[None], jnp.exp(scores - block_top[..., None]), 0.0).astype(jnp.bfloat16)
            weights_wide = weights.astype(jnp.float32)
            block_mass = lax.optimization_barrier(jnp.sum(weights_wide, axis=3))
            block_out = jnp.einsum('hrkb,kbd->hrkd', weights_wide, value_part, precision=lax.Precision.HIGHEST)
            row_top = lax.optimization_barrier(jnp.max(block_top, axis=2))
            factor = jnp.exp(block_top - row_top[..., None])
            numerator = lax.optimization_barrier(jnp.sum(block_out * factor[..., None], axis=2))
            denominator = lax.optimization_barrier(jnp.sum(block_mass * factor, axis=2))
            mixed = numerator / denominator[..., None]
            return jnp.transpose(mixed, (1, 0, 2)).reshape(BLOCK, H * DH)
        first_blk = group * group_rows // BLOCK
        outs_group = lax.map(one_block, jnp.arange(first_blk, end_blk, dtype=jnp.int32))
        pieces.append(outs_group.reshape(group_rows, H * DH))
    return jnp.concatenate(pieces, axis=0)
```

```python
import functools
import math

import jax
import jax.numpy as jnp
from jax import lax
from jax.experimental import pallas as pl
from jax.experimental.pallas import tpu as pltpu
from jax.sharding import Mesh
from jax.sharding import PartitionSpec as P

H = 4
DH = 128
BLOCK = 128
ROWS = 64
COLS = H * ROWS
NEG_FILL = -1e30
EXP2_SCALE = math.log2(math.e) / math.sqrt(DH)

AXES = ("zl", "yh", "yl", "zh", "x", "core")
SIZES = (2, 4, 2, 4, 4, 2)
Q_AXES = ("zl", "x", "core")
KV_AXES = ("zh", "yh", "yl")
N_OWN = 16
N_QB = N_OWN // 2
N_KB = 16
N_PAIR = N_QB * N_KB
EXT = DH + 16

F32 = jnp.float32
BF16 = jnp.bfloat16


def plan_kernel(table_ref, pairs_ref):
    yh, yl = lax.axis_index("yh"), lax.axis_index("yl")
    zh, x, zl = lax.axis_index("zh"), lax.axis_index("x"), lax.axis_index("zl")
    core = lax.axis_index("core")
    q_base = (yh * 2 + yl) * 16 + zh * 4
    k_base = x * 16 + core * 8 + zl * 4

    def one(i, counts):
        full, diag = counts
        kb, qb = i // N_QB, i % N_QB
        key_block = (kb // 4) * 64 + k_base + kb % 4
        query_block = (qb // 4) * 128 + q_base + qb % 4
        listed = (table_ref[qb, key_block] == 1) & (key_block <= query_block)
        on_diag = key_block == query_block

        @pl.when(listed & jnp.logical_not(on_diag))
        def _():
            pairs_ref[2 + full] = i

        @pl.when(listed & on_diag)
        def _():
            pairs_ref[N_PAIR + 1 - diag] = i

        full = full + jnp.where(listed & jnp.logical_not(on_diag), 1, 0)
        diag = diag + jnp.where(listed & on_diag, 1, 0)
        return full, diag

    full, diag = lax.fori_loop(0, N_PAIR, one, (jnp.int32(0), jnp.int32(0)))
    pairs_ref[0] = full
    pairs_ref[1] = diag


def split3(x):
    hi = x.astype(BF16)
    rest = x - hi.astype(F32)
    mid = rest.astype(BF16)
    low = (rest - mid.astype(F32)).astype(BF16)
    return hi, mid, low


def attend_kernel(pairs_ref, q_ref, kv_ref, out_ref, vt_ref, acc_ref, top_ref, *, unroll):
    ones = jnp.ones((EXT - DH, BLOCK), BF16)
    for b in range(N_KB):
        vt_ref[b, :DH, :] = kv_ref[b, :, DH:].T
        vt_ref[b, DH:, :] = ones
    acc_ref[...] = jnp.zeros_like(acc_ref)
    top_ref[...] = jnp.full_like(top_ref, NEG_FILL)

    def units(entries, diagonal):
        work = []
        for entry in entries:
            kb, qb = entry // N_QB, entry % N_QB
            for half in range(2):
                work.append((kb, 2 * qb + half, half))
        scores = [
            jnp.dot(kv_ref[kb, :, :DH], q_ref[own], preferred_element_type=F32)
            for kb, own, _ in work
        ]
        if diagonal:
            key_at = lax.broadcasted_iota(jnp.int32, (BLOCK, COLS), 0)
            row_at = lax.broadcasted_iota(jnp.int32, (BLOCK, COLS), 1) % ROWS
            scores = [
                jnp.where(key_at <= row_at + half * ROWS, s, NEG_FILL)
                for s, (_, _, half) in zip(scores, work)
            ]
        tops = [jnp.max(s, axis=0, keepdims=True) for s in scores]
        weights = [
            jnp.exp2((s - t) * EXP2_SCALE).astype(BF16) for s, t in zip(scores, tops)
        ]
        parts = [
            jnp.dot(vt_ref[kb], w, preferred_element_type=F32)
            for w, (kb, _, _) in zip(weights, work)
        ]
        for part, top, (_, own, _) in zip(parts, tops, work):
            before = top_ref[own]
            after = jnp.maximum(before, top)
            keep = jnp.exp2((before - after) * EXP2_SCALE)
            take = jnp.exp2((top - after) * EXP2_SCALE)
            acc_ref[own] = acc_ref[own] * keep + part * take
            top_ref[own] = after

    full, diag = pairs_ref[0], pairs_ref[1]
    rounds = full // unroll

    def several(i, _):
        units([pairs_ref[2 + i * unroll + k] for k in range(unroll)], False)
        return 0

    def single(i, _):
        units([pairs_ref[2 + rounds * unroll + i]], False)
        return 0

    def on_diagonal(i, _):
        units([pairs_ref[N_PAIR + 1 - i]], True)
        return 0

    lax.fori_loop(0, rounds, several, 0)
    lax.fori_loop(0, full - rounds * unroll, single, 0)
    lax.fori_loop(0, diag, on_diagonal, 0)

    def finish(own, _):
        out_ref[own, :DH, :] = acc_ref[own, :DH, :].astype(BF16)
        mass = split3(acc_ref[own, DH : DH + 1, :])
        top = split3(top_ref[own])
        fill = jnp.zeros((EXT - DH - 6, COLS), BF16)
        out_ref[own, DH:, :] = jnp.concatenate((*mass, *top, fill), axis=0)
        return 0

    lax.fori_loop(0, N_OWN, finish, 0)


def merge_kernel(parts_ref, out_ref):
    def stat(own, at):
        pieces = parts_ref[own, DH:, :].astype(F32)
        return pieces[at : at + 1] + pieces[at + 1 : at + 2] + pieces[at + 2 : at + 3]

    tops = [stat(own, 3) for own in range(N_OWN)]
    highest = functools.reduce(jnp.maximum, tops)
    factors = [jnp.exp2((t - highest) * EXP2_SCALE) for t in tops]
    total = sum(f * stat(own, 0) for own, f in enumerate(factors))
    mixed = sum(f * parts_ref[own, :DH, :].astype(F32) for own, f in enumerate(factors))
    turned = (mixed / total).T
    for h in range(H):
        out_ref[:, h * DH : (h + 1) * DH] = turned[h * ROWS : (h + 1) * ROWS, :]


VMEM = pl.BlockSpec(memory_space=pltpu.VMEM)
SMEM = pl.BlockSpec(memory_space=pltpu.SMEM)


def from_everyone(shard, axes, count):
    copies = jnp.broadcast_to(shard[None], (count, *shard.shape))
    return lax.all_to_all(copies, axes, split_axis=0, concat_axis=0, tiled=True)


def shards(queries, keys, values, block_mask):
    kv = from_everyone(jnp.concatenate((keys, values), axis=1), KV_AXES, 2 * N_KB)
    kv = kv.reshape(N_KB, BLOCK, 2 * DH)

    turned = queries.reshape(ROWS, H, DH).transpose(2, 1, 0).reshape(DH, COLS)
    gathered = from_everyone(turned, Q_AXES, N_OWN)

    line = (lax.axis_index("yh") * 2 + lax.axis_index("yl")) * 4 + lax.axis_index("zh")
    table = lax.dynamic_index_in_dim(
        block_mask.reshape(2, 32, 4, 256), line, 1, keepdims=False
    ).reshape(N_QB, 256)
    pairs = pl.pallas_call(
        plan_kernel,
        out_shape=jax.ShapeDtypeStruct((N_PAIR + 2,), jnp.int32),
        in_specs=[SMEM],
        out_specs=SMEM,
        name="plan",
    )(table)

    parts = pl.pallas_call(
        functools.partial(attend_kernel, unroll=2),
        out_shape=jax.ShapeDtypeStruct((N_OWN, EXT, COLS), BF16),
        in_specs=[SMEM, VMEM, VMEM],
        out_specs=VMEM,
        scratch_shapes=[
            pltpu.VMEM((N_KB, EXT, BLOCK), BF16),
            pltpu.VMEM((N_OWN, EXT, COLS), F32),
            pltpu.VMEM((N_OWN, 1, COLS), F32),
        ],
        name="attend",
    )(pairs, gathered, kv)

    parts = lax.all_to_all(parts, Q_AXES, split_axis=0, concat_axis=0, tiled=True)
    return pl.pallas_call(
        merge_kernel,
        out_shape=jax.ShapeDtypeStruct((ROWS, H * DH), F32),
        in_specs=[VMEM],
        out_specs=VMEM,
        name="merge",
    )(parts)


def solution(mesh):
    fine = Mesh(mesh.devices.reshape(SIZES), AXES)
    by_query = P(AXES, None)
    by_key = P(("zh", "x", "core", "zl", "yh", "yl"), None)
    return jax.shard_map(
        shards,
        mesh=fine,
        in_specs=(by_query, by_key, by_key, P()),
        out_specs=by_query,
        check_vma=False,
    )
```

```python
import functools
import math

import jax
import jax.numpy as jnp
from jax import lax
from jax.experimental import pallas as pl
from jax.experimental.pallas import tpu as pltpu
from jax.sharding import Mesh
from jax.sharding import PartitionSpec as P

H = 4
DH = 128
BLOCK = 128
ROWS = 64
COLS = H * ROWS
NEG_FILL = -1e30
EXP2_SCALE = math.log2(math.e) / math.sqrt(DH)

AXES = ("zl", "yh", "yl", "zh", "x", "core")
SIZES = (2, 4, 2, 4, 4, 2)
Q_AXES = ("x", "zl")
KV_AXES = ("zh", "yh", "yl")
N_OWN = 8
N_KB = 16
N_PAIR = N_OWN * N_KB
LIST = N_PAIR + 8
EXT = DH + 16

F32 = jnp.float32
BF16 = jnp.bfloat16


def plan_kernel(table_ref, pairs_ref):
    yh, yl = lax.axis_index("yh"), lax.axis_index("yl")
    zh, x, zl = lax.axis_index("zh"), lax.axis_index("x"), lax.axis_index("zl")
    core = lax.axis_index("core")
    q_base = (yh * 2 + yl) * 16 + zh * 4
    for side in range(2):
        k_base = x * 16 + (core if side == 0 else 1 - core) * 8 + zl * 4
        full, diag = jnp.int32(0), jnp.int32(0)
        for i in range(N_PAIR):
            kb, own = i // N_OWN, i % N_OWN
            key_block = k_base + (kb // 4) * 64 + kb % 4
            query_block = q_base + (own % 2) * 128 + own // 2
            listed = table_ref[(own % 2) * 4 + own // 2, key_block]
            on_diag = jnp.where(key_block == query_block, listed, 0)
            pairs_ref[side, 2 + full] = jnp.int32(i)
            pairs_ref[side, LIST - 1 - diag] = jnp.int32(i)
            full = full + (listed - on_diag)
            diag = diag + on_diag
        pairs_ref[side, 0] = full
        pairs_ref[side, 1] = diag


def split3(x):
    hi = x.astype(BF16)
    rest = x - hi.astype(F32)
    mid = rest.astype(BF16)
    low = (rest - mid.astype(F32)).astype(BF16)
    return hi, mid, low


def attend_kernel(side, unroll, pairs_ref, q_ref, kv_ref, *refs):
    if side == 0:
        acc_ref, top_ref, vt_ref = refs
    else:
        acc_before_ref, top_before_ref, out_ref, vt_ref, acc_ref, top_ref = refs
    ones = jnp.ones((EXT - DH, BLOCK), BF16)
    for b in range(N_KB):
        vt_ref[b, :DH, :] = kv_ref[b, :, DH:].T
        vt_ref[b, DH:, :] = ones
    acc_ref[...] = jnp.zeros_like(acc_ref)
    top_ref[...] = jnp.full_like(top_ref, NEG_FILL)

    def units(entries, diagonal):
        work = [(entry // N_OWN, entry % N_OWN) for entry in entries]
        scores = [
            jnp.dot(kv_ref[kb, :, :DH], q_ref[own], preferred_element_type=F32)
            for kb, own in work
        ]
        if diagonal:
            first = lax.axis_index("core") * ROWS
            key_at = lax.broadcasted_iota(jnp.int32, (BLOCK, COLS), 0)
            row_at = lax.broadcasted_iota(jnp.int32, (BLOCK, COLS), 1) % ROWS
            scores = [jnp.where(key_at <= row_at + first, s, NEG_FILL) for s in scores]
        tops = [jnp.max(s, axis=0, keepdims=True) for s in scores]
        weights = [
            jnp.exp2((s - t) * EXP2_SCALE).astype(BF16) for s, t in zip(scores, tops)
        ]
        parts = [
            jnp.dot(vt_ref[kb], w, preferred_element_type=F32)
            for w, (kb, _) in zip(weights, work)
        ]
        for part, top, (_, own) in zip(parts, tops, work):
            before = top_ref[own]
            after = jnp.maximum(before, top)
            keep = jnp.exp2((before - after) * EXP2_SCALE)
            take = jnp.exp2((top - after) * EXP2_SCALE)
            acc_ref[own] = acc_ref[own] * keep + part * take
            top_ref[own] = after

    full, diag = pairs_ref[side, 0], pairs_ref[side, 1]
    rounds = full // unroll

    def several(i, _):
        units([pairs_ref[side, 2 + i * unroll + k] for k in range(unroll)], False)
        return 0

    def single(i, _):
        units([pairs_ref[side, 2 + rounds * unroll + i]], False)
        return 0

    def on_diagonal(i, _):
        units([pairs_ref[side, LIST - 1 - i]], True)
        return 0

    lax.fori_loop(0, rounds, several, 0)
    lax.fori_loop(0, full - rounds * unroll, single, 0)
    lax.fori_loop(0, diag, on_diagonal, 0)
    if side == 0:
        return

    def finish(own, _):
        one, two = top_ref[own], top_before_ref[own]
        top = jnp.maximum(one, two)
        acc = acc_ref[own] * jnp.exp2((one - top) * EXP2_SCALE)
        acc = acc + acc_before_ref[own] * jnp.exp2((two - top) * EXP2_SCALE)
        out_ref[own, :DH, :] = acc[:DH].astype(BF16)
        fill = jnp.zeros((EXT - DH - 6, COLS), BF16)
        pieces = (*split3(acc[DH : DH + 1]), *split3(top), fill)
        out_ref[own, DH:, :] = jnp.concatenate(pieces, axis=0)
        return 0

    lax.fori_loop(0, N_OWN, finish, 0)


def merge_kernel(parts_ref, out_ref):
    def stat(own, at):
        pieces = parts_ref[own, DH:, :].astype(F32)
        return pieces[at : at + 1] + pieces[at + 1 : at + 2] + pieces[at + 2 : at + 3]

    tops = [stat(own, 3) for own in range(N_OWN)]
    highest = functools.reduce(jnp.maximum, tops)
    factors = [jnp.exp2((t - highest) * EXP2_SCALE) for t in tops]
    total = sum(f * stat(own, 0) for own, f in enumerate(factors))
    mixed = sum(f * parts_ref[own, :DH, :].astype(F32) for own, f in enumerate(factors))
    turned = (mixed / total).T
    for h in range(H):
        out_ref[:, h * DH : (h + 1) * DH] = turned[h * ROWS : (h + 1) * ROWS, :]


VMEM = pl.BlockSpec(memory_space=pltpu.VMEM)
SMEM = pl.BlockSpec(memory_space=pltpu.SMEM)


def call(kernel, name, out_shape, in_specs, scratch=(), out_specs=VMEM, flops=0):
    return pl.pallas_call(
        kernel,
        out_shape=out_shape,
        in_specs=in_specs,
        out_specs=out_specs,
        scratch_shapes=scratch,
        compiler_params=pltpu.CompilerParams(vmem_limit_bytes=16 << 20),
        cost_estimate=pl.CostEstimate(
            flops=flops, bytes_accessed=4 << 20, transcendentals=flops // 512
        ),
        name=name,
    )


def shards(queries, keys, values, block_mask):
    kv = jnp.concatenate((keys, values), axis=1)
    kv = jnp.broadcast_to(kv[None], (2 * N_KB, ROWS, 2 * DH))
    kv = lax.all_to_all(kv, KV_AXES, split_axis=0, concat_axis=0, tiled=True)
    kv = kv.reshape(N_KB, BLOCK, 2 * DH)

    turned = queries.reshape(ROWS, H, DH).transpose(2, 1, 0).reshape(DH, COLS)
    gathered = lax.all_gather(turned, "zl", axis=0, tiled=True)
    gathered = lax.all_gather(gathered, "x", axis=0, tiled=True)
    gathered = gathered.reshape(N_OWN, DH, COLS)

    line = (lax.axis_index("yh") * 2 + lax.axis_index("yl")) * 4 + lax.axis_index("zh")
    table = lax.dynamic_index_in_dim(
        block_mask.reshape(2, 32, 4, 256), line, 1, keepdims=False
    ).reshape(N_OWN, 256)
    pairs = call(
        plan_kernel,
        "plan",
        jax.ShapeDtypeStruct((2, LIST), jnp.int32),
        [SMEM],
        out_specs=SMEM,
    )(table)

    kv, gathered, pairs = lax.optimization_barrier((kv, gathered, pairs))
    kv_other = lax.ppermute(kv, "core", [(0, 1), (1, 0)])
    acc_shape, top_shape = (N_OWN, EXT, COLS), (N_OWN, 1, COLS)
    turned_values = pltpu.VMEM((N_KB, EXT, BLOCK), BF16)
    acc, top = call(
        functools.partial(attend_kernel, 0, 2),
        "attend_own",
        (jax.ShapeDtypeStruct(acc_shape, F32), jax.ShapeDtypeStruct(top_shape, F32)),
        [SMEM, VMEM, VMEM],
        scratch=[turned_values],
        out_specs=(VMEM, VMEM),
        flops=4 << 30,
    )(pairs, gathered, kv)
    parts = call(
        functools.partial(attend_kernel, 1, 2),
        "attend_other",
        jax.ShapeDtypeStruct(acc_shape, BF16),
        [SMEM] + [VMEM] * 4,
        scratch=[turned_values, pltpu.VMEM(acc_shape, F32), pltpu.VMEM(top_shape, F32)],
        flops=4 << 30,
    )(pairs, gathered, kv_other, acc, top)

    parts = lax.all_to_all(parts, Q_AXES, split_axis=0, concat_axis=0, tiled=True)
    return call(
        merge_kernel, "merge", jax.ShapeDtypeStruct((ROWS, H * DH), F32), [VMEM]
    )(parts)


def solution(mesh):
    fine = Mesh(mesh.devices.reshape(SIZES), AXES)
    by_query = P(AXES, None)
    by_key = P(("zh", "x", "core", "zl", "yh", "yl"), None)
    return jax.shard_map(
        shards,
        mesh=fine,
        in_specs=(by_query, by_key, by_key, P()),
        out_specs=by_query,
        check_vma=False,
    )
```

```python
import functools
import math

import jax
import jax.numpy as jnp
from jax import lax
from jax.experimental import pallas as pl
from jax.experimental.pallas import tpu as pltpu
from jax.sharding import Mesh
from jax.sharding import PartitionSpec as P

H = 4
DH = 128
BLOCK = 128
ROWS = 64
COLS = H * ROWS
NEG_FILL = -1e30
EXP2_SCALE = math.log2(math.e) / math.sqrt(DH)

AXES = ("zl", "yh", "yl", "zh", "x", "core")
SIZES = (2, 4, 2, 4, 4, 2)
Q_AXES = ("zl", "x")
KV_AXES = ("zh", "yh", "yl")
N_OWN = 8
N_KB = 16
N_PAIR = N_OWN * N_KB
LIST = N_PAIR + 8
EXT = DH + 16

F32 = jnp.float32
BF16 = jnp.bfloat16


def plan_kernel(table_ref, pairs_ref):
    yh, yl = lax.axis_index("yh"), lax.axis_index("yl")
    zh, x, zl = lax.axis_index("zh"), lax.axis_index("x"), lax.axis_index("zl")
    core = lax.axis_index("core")
    q_base = (yh * 2 + yl) * 16 + zh * 4
    for side in range(2):
        k_base = x * 16 + (core if side == 0 else 1 - core) * 8 + zl * 4
        full, diag = jnp.int32(0), jnp.int32(0)
        for i in range(N_PAIR):
            kb, own = i // N_OWN, i % N_OWN
            key_block = k_base + (kb // 4) * 64 + kb % 4
            query_block = q_base + (own // 4) * 128 + own % 4
            listed = table_ref[own, key_block]
            on_diag = jnp.where(key_block == query_block, listed, 0)
            pairs_ref[side, 2 + full] = jnp.int32(i)
            pairs_ref[side, LIST - 1 - diag] = jnp.int32(i)
            full = full + (listed - on_diag)
            diag = diag + on_diag
        pairs_ref[side, 0] = full
        pairs_ref[side, 1] = diag


def split3(x):
    hi = x.astype(BF16)
    rest = x - hi.astype(F32)
    mid = rest.astype(BF16)
    low = (rest - mid.astype(F32)).astype(BF16)
    return hi, mid, low


def attend_kernel(side, unroll, pairs_ref, q_ref, kv_ref, *refs):
    if side == 0:
        acc_ref, top_ref, vt_ref = refs
    else:
        acc_before_ref, top_before_ref, out_ref, vt_ref, acc_ref, top_ref = refs
    ones = jnp.ones((EXT - DH, BLOCK), BF16)
    for b in range(N_KB):
        vt_ref[b, :DH, :] = kv_ref[b, :, DH:].T
        vt_ref[b, DH:, :] = ones
    acc_ref[...] = jnp.zeros_like(acc_ref)
    top_ref[...] = jnp.full_like(top_ref, NEG_FILL)

    def units(entries, diagonal):
        work = [(entry // N_OWN, entry % N_OWN) for entry in entries]
        scores = [
            jnp.dot(kv_ref[kb, :, :DH], q_ref[own], preferred_element_type=F32)
            for kb, own in work
        ]
        if diagonal:
            first = lax.axis_index("core") * ROWS
            key_at = lax.broadcasted_iota(jnp.int32, (BLOCK, COLS), 0)
            row_at = lax.broadcasted_iota(jnp.int32, (BLOCK, COLS), 1) % ROWS
            scores = [jnp.where(key_at <= row_at + first, s, NEG_FILL) for s in scores]
        tops = [jnp.max(s, axis=0, keepdims=True) for s in scores]
        weights = [
            jnp.exp2((s - t) * EXP2_SCALE).astype(BF16) for s, t in zip(scores, tops)
        ]
        parts = [
            jnp.dot(vt_ref[kb], w, preferred_element_type=F32)
            for w, (kb, _) in zip(weights, work)
        ]
        for part, top, (_, own) in zip(parts, tops, work):
            before = top_ref[own]
            after = jnp.maximum(before, top)
            keep = jnp.exp2((before - after) * EXP2_SCALE)
            take = jnp.exp2((top - after) * EXP2_SCALE)
            acc_ref[own] = acc_ref[own] * keep + part * take
            top_ref[own] = after

    full, diag = pairs_ref[side, 0], pairs_ref[side, 1]
    rounds = full // unroll

    def several(i, _):
        units([pairs_ref[side, 2 + i * unroll + k] for k in range(unroll)], False)
        return 0

    def single(i, _):
        units([pairs_ref[side, 2 + rounds * unroll + i]], False)
        return 0

    def on_diagonal(i, _):
        units([pairs_ref[side, LIST - 1 - i]], True)
        return 0

    lax.fori_loop(0, rounds, several, 0)
    lax.fori_loop(0, full - rounds * unroll, single, 0)
    lax.fori_loop(0, diag, on_diagonal, 0)
    if side == 0:
        return

    def finish(own, _):
        one, two = top_ref[own], top_before_ref[own]
        top = jnp.maximum(one, two)
        acc = acc_ref[own] * jnp.exp2((one - top) * EXP2_SCALE)
        acc = acc + acc_before_ref[own] * jnp.exp2((two - top) * EXP2_SCALE)
        out_ref[own, :DH, :] = acc[:DH].astype(BF16)
        fill = jnp.zeros((EXT - DH - 6, COLS), BF16)
        pieces = (*split3(acc[DH : DH + 1]), *split3(top), fill)
        out_ref[own, DH:, :] = jnp.concatenate(pieces, axis=0)
        return 0

    lax.fori_loop(0, N_OWN, finish, 0)


def merge_kernel(parts_ref, out_ref):
    def stat(own, at):
        pieces = parts_ref[own, DH:, :].astype(F32)
        return pieces[at : at + 1] + pieces[at + 1 : at + 2] + pieces[at + 2 : at + 3]

    tops = [stat(own, 3) for own in range(N_OWN)]
    highest = functools.reduce(jnp.maximum, tops)
    factors = [jnp.exp2((t - highest) * EXP2_SCALE) for t in tops]
    total = sum(f * stat(own, 0) for own, f in enumerate(factors))
    mixed = sum(f * parts_ref[own, :DH, :].astype(F32) for own, f in enumerate(factors))
    turned = (mixed / total).T
    for h in range(H):
        out_ref[:, h * DH : (h + 1) * DH] = turned[h * ROWS : (h + 1) * ROWS, :]


VMEM = pl.BlockSpec(memory_space=pltpu.VMEM)
SMEM = pl.BlockSpec(memory_space=pltpu.SMEM)


def call(kernel, name, out_shape, in_specs, scratch=(), out_specs=VMEM, flops=0):
    return pl.pallas_call(
        kernel,
        out_shape=out_shape,
        in_specs=in_specs,
        out_specs=out_specs,
        scratch_shapes=scratch,
        compiler_params=pltpu.CompilerParams(vmem_limit_bytes=16 << 20),
        cost_estimate=pl.CostEstimate(
            flops=flops, bytes_accessed=4 << 20, transcendentals=flops // 512
        ),
        name=name,
    )


def shards(queries, keys, values, block_mask):
    kv = jnp.concatenate((keys, values), axis=1)
    kv = jnp.broadcast_to(kv[None], (2 * N_KB, ROWS, 2 * DH))
    kv = lax.all_to_all(kv, KV_AXES, split_axis=0, concat_axis=0, tiled=True)
    kv = kv.reshape(N_KB, BLOCK, 2 * DH)

    turned = queries.reshape(ROWS, H, DH).transpose(2, 1, 0).reshape(DH, COLS)
    gathered = lax.all_gather(turned, "x", axis=0, tiled=True)
    gathered = lax.all_gather(gathered, "zl", axis=0, tiled=True)
    gathered = gathered.reshape(N_OWN, DH, COLS)

    line = (lax.axis_index("yh") * 2 + lax.axis_index("yl")) * 4 + lax.axis_index("zh")
    table = lax.dynamic_index_in_dim(
        block_mask.reshape(2, 32, 4, 256), line, 1, keepdims=False
    ).reshape(N_OWN, 256)
    pairs = call(
        plan_kernel,
        "plan",
        jax.ShapeDtypeStruct((2, LIST), jnp.int32),
        [SMEM],
        out_specs=SMEM,
    )(table)

    kv, gathered, pairs = lax.optimization_barrier((kv, gathered, pairs))
    kv_other = lax.ppermute(kv, "core", [(0, 1), (1, 0)])
    acc_shape, top_shape = (N_OWN, EXT, COLS), (N_OWN, 1, COLS)
    turned_values = pltpu.VMEM((N_KB, EXT, BLOCK), BF16)
    acc, top = call(
        functools.partial(attend_kernel, 0, 2),
        "attend_own",
        (jax.ShapeDtypeStruct(acc_shape, F32), jax.ShapeDtypeStruct(top_shape, F32)),
        [SMEM, VMEM, VMEM],
        scratch=[turned_values],
        out_specs=(VMEM, VMEM),
        flops=4 << 30,
    )(pairs, gathered, kv)
    parts = call(
        functools.partial(attend_kernel, 1, 2),
        "attend_other",
        jax.ShapeDtypeStruct(acc_shape, BF16),
        [SMEM] + [VMEM] * 4,
        scratch=[turned_values, pltpu.VMEM(acc_shape, F32), pltpu.VMEM(top_shape, F32)],
        flops=4 << 30,
    )(pairs, gathered, kv_other, acc, top)

    parts = lax.all_to_all(parts, Q_AXES, split_axis=0, concat_axis=0, tiled=True)
    return call(
        merge_kernel, "merge", jax.ShapeDtypeStruct((ROWS, H * DH), F32), [VMEM]
    )(parts)


def solution(mesh):
    fine = Mesh(mesh.devices.reshape(SIZES), AXES)
    by_query = P(AXES, None)
    by_key = P(("zh", "x", "core", "zl", "yh", "yl"), None)
    return jax.shard_map(
        shards,
        mesh=fine,
        in_specs=(by_query, by_key, by_key, P()),
        out_specs=by_query,
        check_vma=False,
    )
```

```python
import functools
import math

import jax
import jax.numpy as jnp
from jax import lax
from jax.experimental import pallas as pl
from jax.experimental.pallas import tpu as pltpu
from jax.sharding import Mesh
from jax.sharding import PartitionSpec as P

H = 4
DH = 128
BLOCK = 128
ROWS = 64
COLS = H * ROWS
NEG_FILL = -1e30
EXP2_SCALE = math.log2(math.e) / math.sqrt(DH)

AXES = ("zl", "yh", "yl", "zh", "x", "core")
SIZES = (2, 4, 2, 4, 4, 2)
Q_AXES = ("zl", "x")
KV_AXES = ("zh", "yh", "yl")
N_OWN = 8
N_KB = 16
N_PAIR = N_OWN * N_KB
LIST = N_PAIR + 8
WIDTHS = (8, 4, 2, 1)
EXT = DH + 16

F32 = jnp.float32
BF16 = jnp.bfloat16


def plan_kernel(table_ref, pairs_ref):
    yh, yl = lax.axis_index("yh"), lax.axis_index("yl")
    zh, x, zl = lax.axis_index("zh"), lax.axis_index("x"), lax.axis_index("zl")
    core = lax.axis_index("core")
    q_base = (yh * 2 + yl) * 16 + zh * 4
    for side in range(2):
        k_base = x * 16 + (core if side == 0 else 1 - core) * 8 + zl * 4
        full, diag = jnp.int32(0), jnp.int32(0)
        for i in range(N_PAIR):
            kb, own = i // N_OWN, i % N_OWN
            key_block = k_base + (kb // 4) * 64 + kb % 4
            query_block = q_base + (own // 4) * 128 + own % 4
            listed = table_ref[own, key_block]
            on_diag = jnp.where(key_block == query_block, listed, 0)
            pairs_ref[side, 2 + full] = jnp.int32(i)
            pairs_ref[side, LIST - 1 - diag] = jnp.int32(i)
            full = full + (listed - on_diag)
            diag = diag + on_diag
        pairs_ref[side, 0] = full
        pairs_ref[side, 1] = diag


def turn_kernel(rows_ref, out_ref):
    heads = [rows_ref[:, h * DH : (h + 1) * DH] for h in range(H)]
    out_ref[...] = jnp.concatenate(heads, axis=0).T


def split3(x):
    hi = x.astype(BF16)
    rest = x - hi.astype(F32)
    mid = rest.astype(BF16)
    low = (rest - mid.astype(F32)).astype(BF16)
    return hi, mid, low


def attend_kernel(side, pairs_ref, q_ref, kv_ref, *refs):
    if side == 0:
        acc_ref, top_ref, vt_ref = refs
    else:
        acc_before_ref, top_before_ref, out_ref, vt_ref, acc_ref, top_ref = refs
    ones = jnp.ones((EXT - DH, BLOCK), BF16)
    for b in range(N_KB):
        vt_ref[b, :DH, :] = kv_ref[b, :, DH:].T
        vt_ref[b, DH:, :] = ones
    acc_ref[...] = jnp.zeros_like(acc_ref)
    top_ref[...] = jnp.full_like(top_ref, NEG_FILL)

    def units(entries, diagonal):
        work = [(entry // N_OWN, entry % N_OWN) for entry in entries]
        scores = [
            jnp.dot(kv_ref[kb, :, :DH], q_ref[own], preferred_element_type=F32)
            for kb, own in work
        ]
        if diagonal:
            first = lax.axis_index("core") * ROWS
            key_at = lax.broadcasted_iota(jnp.int32, (BLOCK, COLS), 0)
            row_at = lax.broadcasted_iota(jnp.int32, (BLOCK, COLS), 1) % ROWS
            scores = [jnp.where(key_at <= row_at + first, s, NEG_FILL) for s in scores]
        tops = [jnp.max(s, axis=0, keepdims=True) for s in scores]
        weights = [
            jnp.exp2((s - t) * EXP2_SCALE).astype(BF16) for s, t in zip(scores, tops)
        ]
        parts = [
            jnp.dot(vt_ref[kb], w, preferred_element_type=F32)
            for w, (kb, _) in zip(weights, work)
        ]
        for part, top, (_, own) in zip(parts, tops, work):
            before = top_ref[own]
            after = jnp.maximum(before, top)
            keep = jnp.exp2((before - after) * EXP2_SCALE)
            take = jnp.exp2((top - after) * EXP2_SCALE)
            acc_ref[own] = acc_ref[own] * keep + part * take
            top_ref[own] = after

    full, diag = pairs_ref[side, 0], pairs_ref[side, 1]
    done = jnp.int32(0)
    for width in WIDTHS:
        rounds = (full - done) // width

        def several(i, start, width=width):
            units([pairs_ref[side, 2 + start + k] for k in range(width)], False)
            return start + width

        done = lax.fori_loop(0, rounds, several, done)

    def on_diagonal(i, _):
        units([pairs_ref[side, LIST - 1 - i]], True)
        return 0

    lax.fori_loop(0, diag, on_diagonal, 0)
    if side == 0:
        return

    def finish(own, _):
        one, two = top_ref[own], top_before_ref[own]
        top = jnp.maximum(one, two)
        acc = acc_ref[own] * jnp.exp2((one - top) * EXP2_SCALE)
        acc = acc + acc_before_ref[own] * jnp.exp2((two - top) * EXP2_SCALE)
        out_ref[own, :DH, :] = acc[:DH].astype(BF16)
        fill = jnp.zeros((EXT - DH - 6, COLS), BF16)
        pieces = (*split3(acc[DH : DH + 1]), *split3(top), fill)
        out_ref[own, DH:, :] = jnp.concatenate(pieces, axis=0)
        return 0

    lax.fori_loop(0, N_OWN, finish, 0)


def merge_kernel(parts_ref, out_ref):
    def stat(own, at):
        pieces = parts_ref[own, DH:, :].astype(F32)
        return pieces[at : at + 1] + pieces[at + 1 : at + 2] + pieces[at + 2 : at + 3]

    tops = [stat(own, 3) for own in range(N_OWN)]
    highest = functools.reduce(jnp.maximum, tops)
    factors = [jnp.exp2((t - highest) * EXP2_SCALE) for t in tops]
    total = sum(f * stat(own, 0) for own, f in enumerate(factors))
    mixed = sum(f * parts_ref[own, :DH, :].astype(F32) for own, f in enumerate(factors))
    turned = (mixed / total).T
    for h in range(H):
        out_ref[:, h * DH : (h + 1) * DH] = turned[h * ROWS : (h + 1) * ROWS, :]


VMEM = pl.BlockSpec(memory_space=pltpu.VMEM)
SMEM = pl.BlockSpec(memory_space=pltpu.SMEM)


def call(kernel, name, out_shape, in_specs, scratch=(), out_specs=VMEM, flops=0):
    return pl.pallas_call(
        kernel,
        out_shape=out_shape,
        in_specs=in_specs,
        out_specs=out_specs,
        scratch_shapes=scratch,
        compiler_params=pltpu.CompilerParams(vmem_limit_bytes=16 << 20),
        cost_estimate=pl.CostEstimate(
            flops=flops, bytes_accessed=4 << 20, transcendentals=flops // 512
        ),
        name=name,
    )


def shards(queries, keys, values, block_mask):
    kv = jnp.concatenate((keys, values), axis=1)
    kv = jnp.broadcast_to(kv[None], (2 * N_KB, ROWS, 2 * DH))
    kv = lax.all_to_all(kv, KV_AXES, split_axis=0, concat_axis=0, tiled=True)
    kv = kv.reshape(N_KB, BLOCK, 2 * DH)

    line = (lax.axis_index("yh") * 2 + lax.axis_index("yl")) * 4 + lax.axis_index("zh")
    table = lax.dynamic_index_in_dim(
        block_mask.reshape(2, 32, 4, 256), line, 1, keepdims=False
    ).reshape(N_OWN, 256)
    pairs = call(
        plan_kernel,
        "plan",
        jax.ShapeDtypeStruct((2, LIST), jnp.int32),
        [SMEM],
        out_specs=SMEM,
    )(table)

    turned = call(
        turn_kernel, "turn", jax.ShapeDtypeStruct((DH, COLS), BF16), [VMEM]
    )(queries)
    gathered = lax.all_gather(turned, "x", axis=0, tiled=True)
    gathered, pairs = lax.optimization_barrier((gathered, pairs))
    gathered = lax.all_gather(gathered, "zl", axis=0, tiled=True)
    gathered = gathered.reshape(N_OWN, DH, COLS)

    kv, gathered, pairs = lax.optimization_barrier((kv, gathered, pairs))
    kv_other = lax.ppermute(kv, "core", [(0, 1), (1, 0)])
    acc_shape, top_shape = (N_OWN, EXT, COLS), (N_OWN, 1, COLS)
    turned_values = pltpu.VMEM((N_KB, EXT, BLOCK), BF16)
    acc, top = call(
        functools.partial(attend_kernel, 0),
        "attend_own",
        (jax.ShapeDtypeStruct(acc_shape, F32), jax.ShapeDtypeStruct(top_shape, F32)),
        [SMEM, VMEM, VMEM],
        scratch=[turned_values],
        out_specs=(VMEM, VMEM),
        flops=4 << 30,
    )(pairs, gathered, kv)
    parts = call(
        functools.partial(attend_kernel, 1),
        "attend_other",
        jax.ShapeDtypeStruct(acc_shape, BF16),
        [SMEM] + [VMEM] * 4,
        scratch=[turned_values, pltpu.VMEM(acc_shape, F32), pltpu.VMEM(top_shape, F32)],
        flops=4 << 30,
    )(pairs, gathered, kv_other, acc, top)

    parts = lax.all_to_all(parts, Q_AXES, split_axis=0, concat_axis=0, tiled=True)
    return call(
        merge_kernel, "merge", jax.ShapeDtypeStruct((ROWS, H * DH), F32), [VMEM]
    )(parts)


def solution(mesh):
    fine = Mesh(mesh.devices.reshape(SIZES), AXES)
    by_query = P(AXES, None)
    by_key = P(("zh", "x", "core", "zl", "yh", "yl"), None)
    return jax.shard_map(
        shards,
        mesh=fine,
        in_specs=(by_query, by_key, by_key, P()),
        out_specs=by_query,
        check_vma=False,
    )
```

```python
import functools
import math

import jax
import jax.numpy as jnp
from jax import lax
from jax.experimental import pallas as pl
from jax.experimental.pallas import tpu as pltpu
from jax.sharding import Mesh
from jax.sharding import PartitionSpec as P

H = 4
DH = 128
BLOCK = 128
ROWS = 64
COLS = H * ROWS
NEG_FILL = -1e30
EXP2_SCALE = math.log2(math.e) / math.sqrt(DH)

AXES = ("zl", "yh", "yl", "zh", "x", "core")
SIZES = (2, 4, 2, 4, 4, 2)
Q_AXES = ("zl", "x")
KV_AXES = ("zh", "yh", "yl")
N_OWN = 8
N_KB = 16
N_PAIR = N_OWN * N_KB
LIST = N_PAIR + 8
WIDTHS = (12, 4, 2, 1)
DIAGONAL_WIDTHS = (8, 1)
EXT = DH + 16

F32 = jnp.float32
BF16 = jnp.bfloat16


def plan_kernel(table_ref, pairs_ref):
    yh, yl = lax.axis_index("yh"), lax.axis_index("yl")
    zh, x, zl = lax.axis_index("zh"), lax.axis_index("x"), lax.axis_index("zl")
    core = lax.axis_index("core")
    q_base = (yh * 2 + yl) * 16 + zh * 4
    for side in range(2):
        k_base = x * 16 + (core if side == 0 else 1 - core) * 8 + zl * 4
        full, diag = jnp.int32(0), jnp.int32(0)
        for i in range(N_PAIR):
            kb, own = i // N_OWN, i % N_OWN
            key_block = k_base + (kb // 4) * 64 + kb % 4
            query_block = q_base + (own // 4) * 128 + own % 4
            listed = table_ref[own, key_block]
            on_diag = jnp.where(key_block == query_block, listed, 0)
            pairs_ref[side, 2 + full] = jnp.int32(i)
            pairs_ref[side, LIST - 1 - diag] = jnp.int32(i)
            full = full + (listed - on_diag)
            diag = diag + on_diag
        pairs_ref[side, 0] = full
        pairs_ref[side, 1] = diag


def turn_kernel(rows_ref, out_ref):
    heads = [rows_ref[:, h * DH : (h + 1) * DH] for h in range(H)]
    out_ref[...] = jnp.concatenate(heads, axis=0).T


def split3(x):
    hi = x.astype(BF16)
    rest = x - hi.astype(F32)
    mid = rest.astype(BF16)
    low = (rest - mid.astype(F32)).astype(BF16)
    return hi, mid, low


def attend_kernel(side, pairs_ref, q_ref, kv_ref, *refs):
    if side == 0:
        acc_ref, top_ref, vt_ref = refs
    else:
        acc_before_ref, top_before_ref, out_ref, vt_ref, acc_ref, top_ref = refs
    ones = jnp.ones((EXT - DH, BLOCK), BF16)
    for b in range(N_KB):
        vt_ref[b, :DH, :] = kv_ref[b, :, DH:].T
        vt_ref[b, DH:, :] = ones
    acc_ref[...] = jnp.zeros_like(acc_ref)
    top_ref[...] = jnp.full_like(top_ref, NEG_FILL)

    def units(entries, diagonal):
        work = [(entry // N_OWN, entry % N_OWN) for entry in entries]
        scores = [
            jnp.dot(kv_ref[kb, :, :DH], q_ref[own], preferred_element_type=F32)
            for kb, own in work
        ]
        if diagonal:
            first = lax.axis_index("core") * ROWS
            key_at = lax.broadcasted_iota(jnp.int32, (BLOCK, COLS), 0)
            row_at = lax.broadcasted_iota(jnp.int32, (BLOCK, COLS), 1) % ROWS
            scores = [jnp.where(key_at <= row_at + first, s, NEG_FILL) for s in scores]
        tops = [jnp.max(s, axis=0, keepdims=True) for s in scores]
        weights = [
            jnp.exp2((s - t) * EXP2_SCALE).astype(BF16) for s, t in zip(scores, tops)
        ]
        parts = [
            jnp.dot(vt_ref[kb], w, preferred_element_type=F32)
            for w, (kb, _) in zip(weights, work)
        ]
        for part, top, (_, own) in zip(parts, tops, work):
            before = top_ref[own]
            after = jnp.maximum(before, top)
            keep = jnp.exp2((before - after) * EXP2_SCALE)
            take = jnp.exp2((top - after) * EXP2_SCALE)
            acc_ref[own] = acc_ref[own] * keep + part * take
            top_ref[own] = after

    full, diag = pairs_ref[side, 0], pairs_ref[side, 1]

    def run(count, widths, entry_at, diagonal):
        done = jnp.int32(0)
        for width in widths:

            def several(i, start, width=width):
                units([entry_at(start + k) for k in range(width)], diagonal)
                return start + width

            done = lax.fori_loop(0, (count - done) // width, several, done)

    run(full, WIDTHS, lambda at: pairs_ref[side, 2 + at], False)
    run(diag, DIAGONAL_WIDTHS, lambda at: pairs_ref[side, LIST - 1 - at], True)
    if side == 0:
        return

    def finish(own, _):
        one, two = top_ref[own], top_before_ref[own]
        top = jnp.maximum(one, two)
        acc = acc_ref[own] * jnp.exp2((one - top) * EXP2_SCALE)
        acc = acc + acc_before_ref[own] * jnp.exp2((two - top) * EXP2_SCALE)
        out_ref[own, :DH, :] = acc[:DH].astype(BF16)
        fill = jnp.zeros((EXT - DH - 6, COLS), BF16)
        pieces = (*split3(acc[DH : DH + 1]), *split3(top), fill)
        out_ref[own, DH:, :] = jnp.concatenate(pieces, axis=0)
        return 0

    lax.fori_loop(0, N_OWN, finish, 0)


def merge_kernel(parts_ref, out_ref):
    def stat(own, at):
        pieces = parts_ref[own, DH:, :].astype(F32)
        return pieces[at : at + 1] + pieces[at + 1 : at + 2] + pieces[at + 2 : at + 3]

    tops = [stat(own, 3) for own in range(N_OWN)]
    highest = functools.reduce(jnp.maximum, tops)
    factors = [jnp.exp2((t - highest) * EXP2_SCALE) for t in tops]
    total = sum(f * stat(own, 0) for own, f in enumerate(factors))
    mixed = sum(f * parts_ref[own, :DH, :].astype(F32) for own, f in enumerate(factors))
    turned = (mixed / total).T
    for h in range(H):
        out_ref[:, h * DH : (h + 1) * DH] = turned[h * ROWS : (h + 1) * ROWS, :]


VMEM = pl.BlockSpec(memory_space=pltpu.VMEM)
SMEM = pl.BlockSpec(memory_space=pltpu.SMEM)


def call(kernel, name, out_shape, in_specs, scratch=(), out_specs=VMEM, flops=0):
    return pl.pallas_call(
        kernel,
        out_shape=out_shape,
        in_specs=in_specs,
        out_specs=out_specs,
        scratch_shapes=scratch,
        compiler_params=pltpu.CompilerParams(vmem_limit_bytes=16 << 20),
        cost_estimate=pl.CostEstimate(
            flops=flops, bytes_accessed=4 << 20, transcendentals=flops // 512
        ),
        name=name,
    )


def shards(queries, keys, values, block_mask):
    kv = jnp.concatenate((keys, values), axis=1)
    kv = jnp.broadcast_to(kv[None], (2 * N_KB, ROWS, 2 * DH))
    kv = lax.all_to_all(kv, KV_AXES, split_axis=0, concat_axis=0, tiled=True)
    kv = kv.reshape(N_KB, BLOCK, 2 * DH)

    line = (lax.axis_index("yh") * 2 + lax.axis_index("yl")) * 4 + lax.axis_index("zh")
    table = lax.dynamic_index_in_dim(
        block_mask.reshape(2, 32, 4, 256), line, 1, keepdims=False
    ).reshape(N_OWN, 256)
    pairs = call(
        plan_kernel,
        "plan",
        jax.ShapeDtypeStruct((2, LIST), jnp.int32),
        [SMEM],
        out_specs=SMEM,
    )(table)

    turned = call(
        turn_kernel, "turn", jax.ShapeDtypeStruct((DH, COLS), BF16), [VMEM]
    )(queries)
    gathered = lax.all_gather(turned, "x", axis=0, tiled=True)
    gathered, pairs = lax.optimization_barrier((gathered, pairs))
    gathered = lax.all_gather(gathered, "zl", axis=0, tiled=True)
    gathered = gathered.reshape(N_OWN, DH, COLS)

    kv, gathered, pairs = lax.optimization_barrier((kv, gathered, pairs))
    kv_other = lax.ppermute(kv, "core", [(0, 1), (1, 0)])
    acc_shape, top_shape = (N_OWN, EXT, COLS), (N_OWN, 1, COLS)
    turned_values = pltpu.VMEM((N_KB, EXT, BLOCK), BF16)
    acc, top = call(
        functools.partial(attend_kernel, 0),
        "attend_own",
        (jax.ShapeDtypeStruct(acc_shape, F32), jax.ShapeDtypeStruct(top_shape, F32)),
        [SMEM, VMEM, VMEM],
        scratch=[turned_values],
        out_specs=(VMEM, VMEM),
        flops=4 << 30,
    )(pairs, gathered, kv)
    parts = call(
        functools.partial(attend_kernel, 1),
        "attend_other",
        jax.ShapeDtypeStruct(acc_shape, BF16),
        [SMEM] + [VMEM] * 4,
        scratch=[turned_values, pltpu.VMEM(acc_shape, F32), pltpu.VMEM(top_shape, F32)],
        flops=4 << 30,
    )(pairs, gathered, kv_other, acc, top)

    parts = lax.all_to_all(parts, Q_AXES, split_axis=0, concat_axis=0, tiled=True)
    return call(
        merge_kernel, "merge", jax.ShapeDtypeStruct((ROWS, H * DH), F32), [VMEM]
    )(parts)


def solution(mesh):
    fine = Mesh(mesh.devices.reshape(SIZES), AXES)
    by_query = P(AXES, None)
    by_key = P(("zh", "x", "core", "zl", "yh", "yl"), None)
    return jax.shard_map(
        shards,
        mesh=fine,
        in_specs=(by_query, by_key, by_key, P()),
        out_specs=by_query,
        check_vma=False,
    )
```

```python
import functools
import math

import jax
import jax.numpy as jnp
from jax import lax
from jax.experimental import pallas as pl
from jax.experimental.pallas import tpu as pltpu
from jax.sharding import Mesh
from jax.sharding import PartitionSpec as P

H = 4
DH = 128
BLOCK = 128
ROWS = 64
COLS = H * ROWS
NEG_FILL = -1e30
EXP2_SCALE = math.log2(math.e) / math.sqrt(DH)

AXES = ("zl", "yh", "yl", "zh", "x", "core")
SIZES = (2, 4, 2, 4, 4, 2)
Q_AXES = ("zl", "x")
KV_AXES = ("zh", "yh", "yl")
N_OWN = 8
N_KB = 16
N_PAIR = N_OWN * N_KB
LIST = N_PAIR + 8
WIDTHS = (12, 4, 2, 1)
DIAGONAL_WIDTHS = (8, 1)
EXT = DH + 8

F32 = jnp.float32
BF16 = jnp.bfloat16


def plan_kernel(table_ref, pairs_ref):
    yh, yl = lax.axis_index("yh"), lax.axis_index("yl")
    zh, x, zl = lax.axis_index("zh"), lax.axis_index("x"), lax.axis_index("zl")
    core = lax.axis_index("core")
    q_base = (yh * 2 + yl) * 16 + zh * 4
    for side in range(2):
        k_base = x * 16 + (core if side == 0 else 1 - core) * 8 + zl * 4
        full, diag = jnp.int32(0), jnp.int32(0)
        for i in range(N_PAIR):
            kb, own = i // N_OWN, i % N_OWN
            key_block = k_base + (kb // 4) * 64 + kb % 4
            query_block = q_base + (own // 4) * 128 + own % 4
            listed = table_ref[own, key_block]
            on_diag = jnp.where(key_block == query_block, listed, 0)
            pairs_ref[side, 2 + full] = jnp.int32(i)
            pairs_ref[side, LIST - 1 - diag] = jnp.int32(i)
            full = full + (listed - on_diag)
            diag = diag + on_diag
        pairs_ref[side, 0] = full
        pairs_ref[side, 1] = diag


def turn_kernel(rows_ref, out_ref):
    heads = [rows_ref[:, h * DH : (h + 1) * DH] for h in range(H)]
    out_ref[...] = jnp.concatenate(heads, axis=0).T


def split3(x):
    hi = x.astype(BF16)
    rest = x - hi.astype(F32)
    mid = rest.astype(BF16)
    low = (rest - mid.astype(F32)).astype(BF16)
    return hi, mid, low


def attend_kernel(side, pairs_ref, q_ref, kv_ref, *refs):
    if side == 0:
        acc_ref, top_ref, vt_ref = refs
    else:
        acc_before_ref, top_before_ref, out_ref, vt_ref, acc_ref, top_ref = refs
    ones = jnp.ones((EXT - DH, BLOCK), BF16)
    for b in range(N_KB):
        vt_ref[b, :DH, :] = kv_ref[b, :, DH:].T
        vt_ref[b, DH:, :] = ones
    if side == 0:
        acc_ref[...] = jnp.zeros_like(acc_ref)
        top_ref[...] = jnp.full_like(top_ref, NEG_FILL)
    else:
        acc_ref[...] = acc_before_ref[...]
        top_ref[...] = top_before_ref[...]

    def units(entries, diagonal):
        work = [(entry // N_OWN, entry % N_OWN) for entry in entries]
        scores = [
            jnp.dot(kv_ref[kb, :, :DH], q_ref[own], preferred_element_type=F32)
            for kb, own in work
        ]
        if diagonal:
            first = lax.axis_index("core") * ROWS
            key_at = lax.broadcasted_iota(jnp.int32, (BLOCK, COLS), 0)
            row_at = lax.broadcasted_iota(jnp.int32, (BLOCK, COLS), 1) % ROWS
            scores = [jnp.where(key_at <= row_at + first, s, NEG_FILL) for s in scores]
        tops = [jnp.max(s, axis=0, keepdims=True) for s in scores]
        weights = [
            jnp.exp2((s - t) * EXP2_SCALE).astype(BF16) for s, t in zip(scores, tops)
        ]
        parts = [
            jnp.dot(vt_ref[kb], w, preferred_element_type=F32)
            for w, (kb, _) in zip(weights, work)
        ]
        for part, top, (_, own) in zip(parts, tops, work):
            before = top_ref[own]
            after = jnp.maximum(before, top)
            keep = jnp.exp2((before - after) * EXP2_SCALE)
            take = jnp.exp2((top - after) * EXP2_SCALE)
            acc_ref[own] = acc_ref[own] * keep + part * take
            top_ref[own] = after

    full, diag = pairs_ref[side, 0], pairs_ref[side, 1]

    def run(count, widths, entry_at, diagonal):
        done = jnp.int32(0)
        for width in widths:

            def several(i, start, width=width):
                units([entry_at(start + k) for k in range(width)], diagonal)
                return start + width

            done = lax.fori_loop(0, (count - done) // width, several, done)

    run(full, WIDTHS, lambda at: pairs_ref[side, 2 + at], False)
    run(diag, DIAGONAL_WIDTHS, lambda at: pairs_ref[side, LIST - 1 - at], True)
    if side == 0:
        return

    def finish(own, _):
        acc = acc_ref[own]
        out_ref[own, :DH, :] = acc[:DH].astype(BF16)
        fill = jnp.zeros((EXT - DH - 6, COLS), BF16)
        pieces = (*split3(acc[DH : DH + 1]), *split3(top_ref[own]), fill)
        out_ref[own, DH:, :] = jnp.concatenate(pieces, axis=0)
        return 0

    lax.fori_loop(0, N_OWN, finish, 0)


def merge_kernel(parts_ref, out_ref):
    def stat(own, at):
        pieces = parts_ref[own, DH:, :].astype(F32)
        return pieces[at : at + 1] + pieces[at + 1 : at + 2] + pieces[at + 2 : at + 3]

    tops = [stat(own, 3) for own in range(N_OWN)]
    highest = functools.reduce(jnp.maximum, tops)
    factors = [jnp.exp2((t - highest) * EXP2_SCALE) for t in tops]
    total = sum(f * stat(own, 0) for own, f in enumerate(factors))
    mixed = sum(f * parts_ref[own, :DH, :].astype(F32) for own, f in enumerate(factors))
    turned = (mixed / total).T
    for h in range(H):
        out_ref[:, h * DH : (h + 1) * DH] = turned[h * ROWS : (h + 1) * ROWS, :]


VMEM = pl.BlockSpec(memory_space=pltpu.VMEM)
SMEM = pl.BlockSpec(memory_space=pltpu.SMEM)


def call(kernel, name, out_shape, in_specs, scratch=(), out_specs=VMEM, flops=0):
    return pl.pallas_call(
        kernel,
        out_shape=out_shape,
        in_specs=in_specs,
        out_specs=out_specs,
        scratch_shapes=scratch,
        compiler_params=pltpu.CompilerParams(vmem_limit_bytes=16 << 20),
        cost_estimate=pl.CostEstimate(
            flops=flops, bytes_accessed=4 << 20, transcendentals=flops // 512
        ),
        name=name,
    )


def shards(queries, keys, values, block_mask):
    kv = jnp.concatenate((keys, values), axis=1)
    kv = jnp.broadcast_to(kv[None], (2 * N_KB, ROWS, 2 * DH))
    kv = lax.all_to_all(kv, KV_AXES, split_axis=0, concat_axis=0, tiled=True)
    kv = kv.reshape(N_KB, BLOCK, 2 * DH)

    line = (lax.axis_index("yh") * 2 + lax.axis_index("yl")) * 4 + lax.axis_index("zh")
    table = lax.dynamic_index_in_dim(
        block_mask.reshape(2, 32, 4, 256), line, 1, keepdims=False
    ).reshape(N_OWN, 256)
    pairs = call(
        plan_kernel,
        "plan",
        jax.ShapeDtypeStruct((2, LIST), jnp.int32),
        [SMEM],
        out_specs=SMEM,
    )(table)

    turned = call(
        turn_kernel, "turn", jax.ShapeDtypeStruct((DH, COLS), BF16), [VMEM]
    )(queries)
    gathered = lax.all_gather(turned, "x", axis=0, tiled=True)
    gathered, pairs = lax.optimization_barrier((gathered, pairs))
    gathered = lax.all_gather(gathered, "zl", axis=0, tiled=True)
    gathered = gathered.reshape(N_OWN, DH, COLS)

    kv, gathered, pairs = lax.optimization_barrier((kv, gathered, pairs))
    kv_other = lax.ppermute(kv, "core", [(0, 1), (1, 0)])
    acc_shape, top_shape = (N_OWN, EXT, COLS), (N_OWN, 1, COLS)
    turned_values = pltpu.VMEM((N_KB, EXT, BLOCK), BF16)
    acc, top = call(
        functools.partial(attend_kernel, 0),
        "attend_own",
        (jax.ShapeDtypeStruct(acc_shape, F32), jax.ShapeDtypeStruct(top_shape, F32)),
        [SMEM, VMEM, VMEM],
        scratch=[turned_values],
        out_specs=(VMEM, VMEM),
        flops=4 << 30,
    )(pairs, gathered, kv)
    parts = call(
        functools.partial(attend_kernel, 1),
        "attend_other",
        jax.ShapeDtypeStruct(acc_shape, BF16),
        [SMEM] + [VMEM] * 4,
        scratch=[turned_values, pltpu.VMEM(acc_shape, F32), pltpu.VMEM(top_shape, F32)],
        flops=4 << 30,
    )(pairs, gathered, kv_other, acc, top)

    parts = lax.all_to_all(parts, Q_AXES, split_axis=0, concat_axis=0, tiled=True)
    return call(
        merge_kernel, "merge", jax.ShapeDtypeStruct((ROWS, H * DH), F32), [VMEM]
    )(parts)


def solution(mesh):
    fine = Mesh(mesh.devices.reshape(SIZES), AXES)
    by_query = P(AXES, None)
    by_key = P(("zh", "x", "core", "zl", "yh", "yl"), None)
    return jax.shard_map(
        shards,
        mesh=fine,
        in_specs=(by_query, by_key, by_key, P()),
        out_specs=by_query,
        check_vma=False,
    )
```

```python
import functools
import math

import jax
import jax.numpy as jnp
from jax import lax
from jax.experimental import pallas as pl
from jax.experimental.pallas import tpu as pltpu
from jax.sharding import Mesh
from jax.sharding import PartitionSpec as P

H = 4
DH = 128
BLOCK = 128
ROWS = 64
COLS = H * ROWS
NEG_FILL = -1e30
EXP2_SCALE = math.log2(math.e) / math.sqrt(DH)

AXES = ("zl", "yh", "yl", "zh", "x", "core")
SIZES = (2, 4, 2, 4, 4, 2)
Q_AXES = ("zl", "x")
KV_AXES = ("zh", "yh", "yl")
N_OWN = 8
N_KB = 16
N_PAIR = N_OWN * N_KB
LIST = N_PAIR + 8
WIDTHS = (12, 4, 2, 1)
DIAGONAL_WIDTHS = (8, 1)
EXT = DH + 8

F32 = jnp.float32
BF16 = jnp.bfloat16


def plan_kernel(table_ref, pairs_ref):
    yh, yl = lax.axis_index("yh"), lax.axis_index("yl")
    zh, x, zl = lax.axis_index("zh"), lax.axis_index("x"), lax.axis_index("zl")
    core = lax.axis_index("core")
    q_base = (yh * 2 + yl) * 16 + zh * 4
    for side in range(2):
        k_base = x * 16 + (core if side == 0 else 1 - core) * 8 + zl * 4
        full, diag = jnp.int32(0), jnp.int32(0)
        for i in range(N_PAIR):
            kb, own = i // N_OWN, i % N_OWN
            key_block = k_base + (kb // 4) * 64 + kb % 4
            query_block = q_base + (own // 4) * 128 + own % 4
            listed = table_ref[own, key_block]
            on_diag = jnp.where(key_block == query_block, listed, 0)
            pairs_ref[side, 2 + full] = jnp.int32(i)
            pairs_ref[side, LIST - 1 - diag] = jnp.int32(i)
            full = full + (listed - on_diag)
            diag = diag + on_diag
        pairs_ref[side, 0] = full
        pairs_ref[side, 1] = diag


def turn_kernel(rows_ref, out_ref):
    heads = [rows_ref[:, h * DH : (h + 1) * DH] for h in range(H)]
    out_ref[...] = jnp.concatenate(heads, axis=0).T


def split3(x):
    hi = x.astype(BF16)
    rest = x - hi.astype(F32)
    mid = rest.astype(BF16)
    low = (rest - mid.astype(F32)).astype(BF16)
    return hi, mid, low


def attend_kernel(side, pairs_ref, q_ref, kv_ref, *refs):
    if side == 0:
        acc_ref, top_ref, vt_ref = refs
    else:
        acc_before_ref, top_before_ref, out_ref, vt_ref, acc_ref, top_ref = refs
    ones = jnp.ones((EXT - DH, BLOCK), BF16)
    for b in range(N_KB):
        vt_ref[b, :DH, :] = kv_ref[b, :, DH:].T
        vt_ref[b, DH:, :] = ones
    if side == 0:
        acc_ref[...] = jnp.zeros_like(acc_ref)
        top_ref[...] = jnp.full_like(top_ref, NEG_FILL)
    else:
        acc_ref[...] = acc_before_ref[...]
        top_ref[...] = top_before_ref[...]

    def units(entries, diagonal):
        work = [(entry // N_OWN, entry % N_OWN) for entry in entries]
        scores = [
            jnp.dot(kv_ref[kb, :, :DH], q_ref[own], preferred_element_type=F32)
            for kb, own in work
        ]
        if diagonal:
            first = lax.axis_index("core") * ROWS
            key_at = lax.broadcasted_iota(jnp.int32, (BLOCK, COLS), 0)
            row_at = lax.broadcasted_iota(jnp.int32, (BLOCK, COLS), 1) % ROWS
            scores = [jnp.where(key_at <= row_at + first, s, NEG_FILL) for s in scores]
        tops = [jnp.max(s, axis=0, keepdims=True) for s in scores]
        weights = [
            jnp.exp2((s - t) * EXP2_SCALE).astype(BF16) for s, t in zip(scores, tops)
        ]
        parts = [
            jnp.dot(vt_ref[kb], w, preferred_element_type=F32)
            for w, (kb, _) in zip(weights, work)
        ]
        for part, top, (_, own) in zip(parts, tops, work):
            before = top_ref[own]
            after = jnp.maximum(before, top)
            keep = jnp.exp2((before - after) * EXP2_SCALE)
            take = jnp.exp2((top - after) * EXP2_SCALE)
            acc_ref[own] = acc_ref[own] * keep + part * take
            top_ref[own] = after

    full, diag = pairs_ref[side, 0], pairs_ref[side, 1]

    def run(count, widths, entry_at, diagonal):
        done = jnp.int32(0)
        for width in widths:

            def several(i, start, width=width):
                units([entry_at(start + k) for k in range(width)], diagonal)
                return start + width

            done = lax.fori_loop(0, (count - done) // width, several, done)

    run(full, WIDTHS, lambda at: pairs_ref[side, 2 + at], False)
    run(diag, DIAGONAL_WIDTHS, lambda at: pairs_ref[side, LIST - 1 - at], True)
    if side == 0:
        return

    for own in range(N_OWN):
        acc = acc_ref[own]
        out_ref[own, :DH, :] = acc[:DH].astype(BF16)
        fill = jnp.zeros((EXT - DH - 6, COLS), BF16)
        pieces = (*split3(acc[DH : DH + 1]), *split3(top_ref[own]), fill)
        out_ref[own, DH:, :] = jnp.concatenate(pieces, axis=0)


def merge_kernel(parts_ref, out_ref):
    def stat(own, at):
        pieces = parts_ref[own, DH:, :].astype(F32)
        return pieces[at : at + 1] + pieces[at + 1 : at + 2] + pieces[at + 2 : at + 3]

    tops = [stat(own, 3) for own in range(N_OWN)]
    highest = functools.reduce(jnp.maximum, tops)
    factors = [jnp.exp2((t - highest) * EXP2_SCALE) for t in tops]
    total = sum(f * stat(own, 0) for own, f in enumerate(factors))
    mixed = sum(f * parts_ref[own, :DH, :].astype(F32) for own, f in enumerate(factors))
    turned = (mixed / total).T
    for h in range(H):
        out_ref[:, h * DH : (h + 1) * DH] = turned[h * ROWS : (h + 1) * ROWS, :]


VMEM = pl.BlockSpec(memory_space=pltpu.VMEM)
SMEM = pl.BlockSpec(memory_space=pltpu.SMEM)


def call(kernel, name, out_shape, in_specs, scratch=(), out_specs=VMEM, flops=0):
    return pl.pallas_call(
        kernel,
        out_shape=out_shape,
        in_specs=in_specs,
        out_specs=out_specs,
        scratch_shapes=scratch,
        compiler_params=pltpu.CompilerParams(vmem_limit_bytes=16 << 20),
        cost_estimate=pl.CostEstimate(
            flops=flops, bytes_accessed=4 << 20, transcendentals=flops // 512
        ),
        name=name,
    )


def shards(queries, keys, values, block_mask):
    kv = jnp.concatenate((keys, values), axis=1)
    kv = jnp.broadcast_to(kv[None], (2 * N_KB, ROWS, 2 * DH))
    kv = lax.all_to_all(kv, KV_AXES, split_axis=0, concat_axis=0, tiled=True)
    kv = kv.reshape(N_KB, BLOCK, 2 * DH)

    line = (lax.axis_index("yh") * 2 + lax.axis_index("yl")) * 4 + lax.axis_index("zh")
    table = lax.dynamic_index_in_dim(
        block_mask.reshape(2, 32, 4, 256), line, 1, keepdims=False
    ).reshape(N_OWN, 256)
    pairs = call(
        plan_kernel,
        "plan",
        jax.ShapeDtypeStruct((2, LIST), jnp.int32),
        [SMEM],
        out_specs=SMEM,
    )(table)

    turned = call(
        turn_kernel, "turn", jax.ShapeDtypeStruct((DH, COLS), BF16), [VMEM]
    )(queries)
    gathered = lax.all_gather(turned, "x", axis=0, tiled=True)
    gathered, pairs = lax.optimization_barrier((gathered, pairs))
    gathered = lax.all_gather(gathered, "zl", axis=0, tiled=True)
    gathered = gathered.reshape(N_OWN, DH, COLS)

    kv, gathered, pairs = lax.optimization_barrier((kv, gathered, pairs))
    kv_other = lax.ppermute(kv, "core", [(0, 1), (1, 0)])
    acc_shape, top_shape = (N_OWN, EXT, COLS), (N_OWN, 1, COLS)
    turned_values = pltpu.VMEM((N_KB, EXT, BLOCK), BF16)
    acc, top = call(
        functools.partial(attend_kernel, 0),
        "attend_own",
        (jax.ShapeDtypeStruct(acc_shape, F32), jax.ShapeDtypeStruct(top_shape, F32)),
        [SMEM, VMEM, VMEM],
        scratch=[turned_values],
        out_specs=(VMEM, VMEM),
        flops=4 << 30,
    )(pairs, gathered, kv)
    parts = call(
        functools.partial(attend_kernel, 1),
        "attend_other",
        jax.ShapeDtypeStruct(acc_shape, BF16),
        [SMEM] + [VMEM] * 4,
        scratch=[turned_values, pltpu.VMEM(acc_shape, F32), pltpu.VMEM(top_shape, F32)],
        flops=4 << 30,
    )(pairs, gathered, kv_other, acc, top)

    parts = lax.all_to_all(parts, Q_AXES, split_axis=0, concat_axis=0, tiled=True)
    return call(
        merge_kernel, "merge", jax.ShapeDtypeStruct((ROWS, H * DH), F32), [VMEM]
    )(parts)


def solution(mesh):
    fine = Mesh(mesh.devices.reshape(SIZES), AXES)
    by_query = P(AXES, None)
    by_key = P(("zh", "x", "core", "zl", "yh", "yl"), None)
    return jax.shard_map(
        shards,
        mesh=fine,
        in_specs=(by_query, by_key, by_key, P()),
        out_specs=by_query,
        check_vma=False,
    )
```

```python
import functools
import math

import jax
import jax.numpy as jnp
from jax import lax
from jax.experimental import pallas as pl
from jax.experimental.pallas import tpu as pltpu
from jax.sharding import Mesh
from jax.sharding import PartitionSpec as P

H = 4
DH = 128
BLOCK = 128
ROWS = 64
COLS = H * ROWS
NEG_FILL = -1e30
EXP2_SCALE = math.log2(math.e) / math.sqrt(DH)

AXES = ("zl", "yh", "yl", "zh", "x", "core")
SIZES = (2, 4, 2, 4, 4, 2)
Q_AXES = ("x", "zl")
KV_AXES = ("zh", "yh", "yl")
N_OWN = 8
N_KB = 16
N_PAIR = N_OWN * N_KB
LIST = N_PAIR + 8
WIDTHS = (12, 4, 2, 1)
DIAGONAL_WIDTHS = (8, 1)
EXT = DH + 8

F32 = jnp.float32
BF16 = jnp.bfloat16


def plan_kernel(table_ref, pairs_ref):
    yh, yl = lax.axis_index("yh"), lax.axis_index("yl")
    zh, x, zl = lax.axis_index("zh"), lax.axis_index("x"), lax.axis_index("zl")
    core = lax.axis_index("core")
    q_base = (yh * 2 + yl) * 16 + zh * 4
    for side in range(2):
        k_base = x * 16 + (core if side == 0 else 1 - core) * 8 + zl * 4
        full, diag = jnp.int32(0), jnp.int32(0)
        for i in range(N_PAIR):
            kb, own = i // N_OWN, i % N_OWN
            row = (zl + own % 2) % 2 * 4 + own // 2
            key_block = k_base + (kb // 4) * 64 + kb % 4
            query_block = q_base + (row // 4) * 128 + row % 4
            listed = table_ref[row, key_block]
            on_diag = jnp.where(key_block == query_block, listed, 0)
            pairs_ref[side, 2 + full] = jnp.int32(i)
            pairs_ref[side, LIST - 1 - diag] = jnp.int32(i)
            full = full + (listed - on_diag)
            diag = diag + on_diag
        pairs_ref[side, 0] = full
        pairs_ref[side, 1] = diag


def turn_kernel(own_ref, other_ref, out_ref):
    for side, rows_ref in enumerate((own_ref, other_ref)):
        heads = [rows_ref[:, h * DH : (h + 1) * DH] for h in range(H)]
        out_ref[side] = jnp.concatenate(heads, axis=0).T


def split3(x):
    hi = x.astype(BF16)
    rest = x - hi.astype(F32)
    mid = rest.astype(BF16)
    low = (rest - mid.astype(F32)).astype(BF16)
    return hi, mid, low


def attend_kernel(side, pairs_ref, q_ref, kv_ref, *refs):
    if side == 0:
        acc_ref, top_ref, vt_ref = refs
    else:
        acc_before_ref, top_before_ref, out_ref, vt_ref, acc_ref, top_ref = refs
    ones = jnp.ones((EXT - DH, BLOCK), BF16)
    for b in range(N_KB):
        vt_ref[b, :DH, :] = kv_ref[b, :, DH:].T
        vt_ref[b, DH:, :] = ones
    if side == 0:
        acc_ref[...] = jnp.zeros_like(acc_ref)
        top_ref[...] = jnp.full_like(top_ref, NEG_FILL)
    else:
        acc_ref[...] = acc_before_ref[...]
        top_ref[...] = top_before_ref[...]

    def units(entries, diagonal):
        work = [(entry // N_OWN, entry % N_OWN) for entry in entries]
        scores = [
            jnp.dot(kv_ref[kb, :, :DH], q_ref[own], preferred_element_type=F32)
            for kb, own in work
        ]
        if diagonal:
            first = lax.axis_index("core") * ROWS
            key_at = lax.broadcasted_iota(jnp.int32, (BLOCK, COLS), 0)
            row_at = lax.broadcasted_iota(jnp.int32, (BLOCK, COLS), 1) % ROWS
            scores = [jnp.where(key_at <= row_at + first, s, NEG_FILL) for s in scores]
        tops = [jnp.max(s, axis=0, keepdims=True) for s in scores]
        weights = [
            jnp.exp2((s - t) * EXP2_SCALE).astype(BF16) for s, t in zip(scores, tops)
        ]
        parts = [
            jnp.dot(vt_ref[kb], w, preferred_element_type=F32)
            for w, (kb, _) in zip(weights, work)
        ]
        for part, top, (_, own) in zip(parts, tops, work):
            before = top_ref[own]
            after = jnp.maximum(before, top)
            keep = jnp.exp2((before - after) * EXP2_SCALE)
            take = jnp.exp2((top - after) * EXP2_SCALE)
            acc_ref[own] = acc_ref[own] * keep + part * take
            top_ref[own] = after

    full, diag = pairs_ref[side, 0], pairs_ref[side, 1]

    def run(count, widths, entry_at, diagonal):
        done = jnp.int32(0)
        for width in widths:

            def several(i, start, width=width):
                units([entry_at(start + k) for k in range(width)], diagonal)
                return start + width

            done = lax.fori_loop(0, (count - done) // width, several, done)

    run(full, WIDTHS, lambda at: pairs_ref[side, 2 + at], False)
    run(diag, DIAGONAL_WIDTHS, lambda at: pairs_ref[side, LIST - 1 - at], True)
    if side == 0:
        return

    for own in range(N_OWN):
        acc = acc_ref[own]
        to = own // 2 * 2 + (own + lax.axis_index("zl")) % 2
        out_ref[to, :DH, :] = acc[:DH].astype(BF16)
        fill = jnp.zeros((EXT - DH - 6, COLS), BF16)
        pieces = (*split3(acc[DH : DH + 1]), *split3(top_ref[own]), fill)
        out_ref[to, DH:, :] = jnp.concatenate(pieces, axis=0)


def merge_kernel(parts_ref, out_ref):
    def stat(own, at):
        pieces = parts_ref[own, DH:, :].astype(F32)
        return pieces[at : at + 1] + pieces[at + 1 : at + 2] + pieces[at + 2 : at + 3]

    tops = [stat(own, 3) for own in range(N_OWN)]
    highest = functools.reduce(jnp.maximum, tops)
    factors = [jnp.exp2((t - highest) * EXP2_SCALE) for t in tops]
    total = sum(f * stat(own, 0) for own, f in enumerate(factors))
    mixed = sum(f * parts_ref[own, :DH, :].astype(F32) for own, f in enumerate(factors))
    turned = (mixed / total).T
    for h in range(H):
        out_ref[:, h * DH : (h + 1) * DH] = turned[h * ROWS : (h + 1) * ROWS, :]


VMEM = pl.BlockSpec(memory_space=pltpu.VMEM)
SMEM = pl.BlockSpec(memory_space=pltpu.SMEM)


def call(kernel, name, out_shape, in_specs, scratch=(), out_specs=VMEM, flops=0):
    return pl.pallas_call(
        kernel,
        out_shape=out_shape,
        in_specs=in_specs,
        out_specs=out_specs,
        scratch_shapes=scratch,
        compiler_params=pltpu.CompilerParams(vmem_limit_bytes=16 << 20),
        cost_estimate=pl.CostEstimate(
            flops=flops, bytes_accessed=4 << 20, transcendentals=flops // 512
        ),
        name=name,
    )


def shards(queries, keys, values, block_mask):
    other = lax.ppermute(queries, "zl", [(0, 1), (1, 0)])
    kv = jnp.concatenate((keys, values), axis=1)
    kv = jnp.broadcast_to(kv[None], (2 * N_KB, ROWS, 2 * DH))
    kv = lax.all_to_all(kv, KV_AXES, split_axis=0, concat_axis=0, tiled=True)
    kv = kv.reshape(N_KB, BLOCK, 2 * DH)

    turned = call(
        turn_kernel, "turn", jax.ShapeDtypeStruct((2, DH, COLS), BF16), [VMEM] * 2
    )(queries, other)
    gathered = lax.all_gather(turned, "x", axis=0, tiled=True)

    mask, gathered = lax.optimization_barrier((block_mask, gathered))
    line = (lax.axis_index("yh") * 2 + lax.axis_index("yl")) * 4 + lax.axis_index("zh")
    table = lax.dynamic_index_in_dim(
        mask.reshape(2, 32, 4, 256), line, 1, keepdims=False
    ).reshape(N_OWN, 256)
    pairs = call(
        plan_kernel,
        "plan",
        jax.ShapeDtypeStruct((2, LIST), jnp.int32),
        [SMEM],
        out_specs=SMEM,
        flops=64 << 30,
    )(table)

    gathered = gathered.reshape(N_OWN, DH, COLS)

    kv, gathered, pairs = lax.optimization_barrier((kv, gathered, pairs))
    kv_other = lax.ppermute(kv, "core", [(0, 1), (1, 0)])
    acc_shape, top_shape = (N_OWN, EXT, COLS), (N_OWN, 1, COLS)
    turned_values = pltpu.VMEM((N_KB, EXT, BLOCK), BF16)
    acc, top = call(
        functools.partial(attend_kernel, 0),
        "attend_own",
        (jax.ShapeDtypeStruct(acc_shape, F32), jax.ShapeDtypeStruct(top_shape, F32)),
        [SMEM, VMEM, VMEM],
        scratch=[turned_values],
        out_specs=(VMEM, VMEM),
        flops=4 << 30,
    )(pairs, gathered, kv)
    parts = call(
        functools.partial(attend_kernel, 1),
        "attend_other",
        jax.ShapeDtypeStruct(acc_shape, BF16),
        [SMEM] + [VMEM] * 4,
        scratch=[turned_values, pltpu.VMEM(acc_shape, F32), pltpu.VMEM(top_shape, F32)],
        flops=4 << 30,
    )(pairs, gathered, kv_other, acc, top)

    parts = lax.all_to_all(parts, Q_AXES, split_axis=0, concat_axis=0, tiled=True)
    return call(
        merge_kernel, "merge", jax.ShapeDtypeStruct((ROWS, H * DH), F32), [VMEM]
    )(parts)


def solution(mesh):
    fine = Mesh(mesh.devices.reshape(SIZES), AXES)
    by_query = P(AXES, None)
    by_key = P(("zh", "x", "core", "zl", "yh", "yl"), None)
    return jax.shard_map(
        shards,
        mesh=fine,
        in_specs=(by_query, by_key, by_key, P()),
        out_specs=by_query,
        check_vma=False,
    )
```

```python
import functools
import math

import jax
import jax.numpy as jnp
from jax import lax
from jax.experimental import pallas as pl
from jax.experimental.pallas import tpu as pltpu
from jax.sharding import Mesh
from jax.sharding import PartitionSpec as P

H = 4
DH = 128
BLOCK = 128
ROWS = 64
COLS = H * ROWS
NEG_FILL = -1e30
EXP2_SCALE = math.log2(math.e) / math.sqrt(DH)

AXES = ("zl", "yh", "yl", "zh", "x", "core")
SIZES = (2, 4, 2, 4, 4, 2)
Q_AXES = ("zl", "x")
KV_AXES = ("zh", "yh", "yl")
N_OWN = 8
N_KB = 16
N_PAIR = N_OWN * N_KB
LIST = N_PAIR + 8
WIDTHS = ((12, 6, 3, 2, 1), (16, 8, 4, 2, 1))
DIAGONAL_WIDTHS = (8, 1)
EXT = DH + 8

F32 = jnp.float32
BF16 = jnp.bfloat16


def plan_kernel(table_ref, pairs_ref):
    yh, yl = lax.axis_index("yh"), lax.axis_index("yl")
    zh, x, zl = lax.axis_index("zh"), lax.axis_index("x"), lax.axis_index("zl")
    core = lax.axis_index("core")
    q_base = (yh * 2 + yl) * 16 + zh * 4
    for side in range(2):
        k_base = x * 16 + (core if side == 0 else 1 - core) * 8 + zl * 4
        full, diag = jnp.int32(0), jnp.int32(0)
        for i in range(N_PAIR):
            kb, own = i // N_OWN, i % N_OWN
            key_block = k_base + (kb // 4) * 64 + kb % 4
            query_block = q_base + (own // 4) * 128 + own % 4
            listed = table_ref[own, key_block]
            on_diag = jnp.where(key_block == query_block, listed, 0)
            pairs_ref[side, 2 + full] = jnp.int32(i)
            pairs_ref[side, LIST - 1 - diag] = jnp.int32(i)
            full = full + (listed - on_diag)
            diag = diag + on_diag
        pairs_ref[side, 0] = full
        pairs_ref[side, 1] = diag


def turn_kernel(rows_ref, out_ref):
    heads = [rows_ref[:, h * DH : (h + 1) * DH] for h in range(H)]
    out_ref[...] = jnp.concatenate(heads, axis=0).T


def split3(x):
    hi = x.astype(BF16)
    rest = x - hi.astype(F32)
    mid = rest.astype(BF16)
    low = (rest - mid.astype(F32)).astype(BF16)
    return hi, mid, low


def attend_kernel(side, pairs_ref, q_ref, kv_ref, *refs):
    if side == 0:
        acc_ref, top_ref, vt_ref = refs
    else:
        acc_before_ref, top_before_ref, out_ref, vt_ref, acc_ref, top_ref = refs
    ones = jnp.ones((EXT - DH, BLOCK), BF16)
    for b in range(N_KB):
        vt_ref[b, :DH, :] = kv_ref[b, :, DH:].T
        vt_ref[b, DH:, :] = ones
    if side == 0:
        acc_ref[...] = jnp.zeros_like(acc_ref)
        top_ref[...] = jnp.full_like(top_ref, NEG_FILL)
    else:
        acc_ref[...] = acc_before_ref[...]
        top_ref[...] = top_before_ref[...]

    def units(entries, diagonal):
        work = [(entry // N_OWN, entry % N_OWN) for entry in entries]
        scores = [
            jnp.dot(kv_ref[kb, :, :DH], q_ref[own], preferred_element_type=F32)
            for kb, own in work
        ]
        if diagonal:
            first = lax.axis_index("core") * ROWS
            key_at = lax.broadcasted_iota(jnp.int32, (BLOCK, COLS), 0)
            row_at = lax.broadcasted_iota(jnp.int32, (BLOCK, COLS), 1) % ROWS
            scores = [jnp.where(key_at <= row_at + first, s, NEG_FILL) for s in scores]
        tops = [jnp.max(s, axis=0, keepdims=True) for s in scores]
        weights = [
            jnp.exp2((s - t) * EXP2_SCALE).astype(BF16) for s, t in zip(scores, tops)
        ]
        parts = [
            jnp.dot(vt_ref[kb], w, preferred_element_type=F32)
            for w, (kb, _) in zip(weights, work)
        ]
        for part, top, (_, own) in zip(parts, tops, work):
            before = top_ref[own]
            after = jnp.maximum(before, top)
            keep = jnp.exp2((before - after) * EXP2_SCALE)
            take = jnp.exp2((top - after) * EXP2_SCALE)
            acc_ref[own] = acc_ref[own] * keep + part * take
            top_ref[own] = after

    full, diag = pairs_ref[side, 0], pairs_ref[side, 1]

    def run(count, widths, entry_at, diagonal):
        done = jnp.int32(0)
        for width in widths:

            def several(i, start, width=width):
                units([entry_at(start + k) for k in range(width)], diagonal)
                return start + width

            done = lax.fori_loop(0, (count - done) // width, several, done)

    run(full, WIDTHS[side], lambda at: pairs_ref[side, 2 + at], False)
    run(diag, DIAGONAL_WIDTHS, lambda at: pairs_ref[side, LIST - 1 - at], True)
    if side == 0:
        return

    for own in range(N_OWN):
        acc = acc_ref[own]
        out_ref[own, :DH, :] = acc[:DH].astype(BF16)
        fill = jnp.zeros((EXT - DH - 6, COLS), BF16)
        pieces = (*split3(acc[DH : DH + 1]), *split3(top_ref[own]), fill)
        out_ref[own, DH:, :] = jnp.concatenate(pieces, axis=0)


def merge_kernel(parts_ref, out_ref):
    def stat(own, at):
        pieces = parts_ref[own, DH:, :].astype(F32)
        return pieces[at : at + 1] + pieces[at + 1 : at + 2] + pieces[at + 2 : at + 3]

    tops = [stat(own, 3) for own in range(N_OWN)]
    highest = functools.reduce(jnp.maximum, tops)
    factors = [jnp.exp2((t - highest) * EXP2_SCALE) for t in tops]
    total = sum(f * stat(own, 0) for own, f in enumerate(factors))
    mixed = sum(f * parts_ref[own, :DH, :].astype(F32) for own, f in enumerate(factors))
    turned = (mixed / total).T
    for h in range(H):
        out_ref[:, h * DH : (h + 1) * DH] = turned[h * ROWS : (h + 1) * ROWS, :]


VMEM = pl.BlockSpec(memory_space=pltpu.VMEM)
SMEM = pl.BlockSpec(memory_space=pltpu.SMEM)


def call(kernel, name, out_shape, in_specs, scratch=(), out_specs=VMEM, flops=0):
    return pl.pallas_call(
        kernel,
        out_shape=out_shape,
        in_specs=in_specs,
        out_specs=out_specs,
        scratch_shapes=scratch,
        compiler_params=pltpu.CompilerParams(vmem_limit_bytes=16 << 20),
        cost_estimate=pl.CostEstimate(
            flops=flops, bytes_accessed=4 << 20, transcendentals=flops // 512
        ),
        name=name,
    )


def shards(queries, keys, values, block_mask):
    kv = jnp.concatenate((keys, values), axis=1)
    kv = jnp.broadcast_to(kv[None], (2 * N_KB, ROWS, 2 * DH))
    kv = lax.all_to_all(kv, KV_AXES, split_axis=0, concat_axis=0, tiled=True)
    kv = kv.reshape(N_KB, BLOCK, 2 * DH)

    line = (lax.axis_index("yh") * 2 + lax.axis_index("yl")) * 4 + lax.axis_index("zh")
    table = lax.dynamic_index_in_dim(
        block_mask.reshape(2, 32, 4, 256), line, 1, keepdims=False
    ).reshape(N_OWN, 256)
    pairs = call(
        plan_kernel,
        "plan",
        jax.ShapeDtypeStruct((2, LIST), jnp.int32),
        [SMEM],
        out_specs=SMEM,
    )(table)

    turned = call(
        turn_kernel, "turn", jax.ShapeDtypeStruct((DH, COLS), BF16), [VMEM]
    )(queries)
    gathered = lax.all_gather(turned, "x", axis=0, tiled=True)
    gathered, pairs = lax.optimization_barrier((gathered, pairs))
    gathered = lax.all_gather(gathered, "zl", axis=0, tiled=True)
    gathered = gathered.reshape(N_OWN, DH, COLS)

    kv, gathered, pairs = lax.optimization_barrier((kv, gathered, pairs))
    kv_other = lax.ppermute(kv, "core", [(0, 1), (1, 0)])
    acc_shape, top_shape = (N_OWN, EXT, COLS), (N_OWN, 1, COLS)
    turned_values = pltpu.VMEM((N_KB, EXT, BLOCK), BF16)
    acc, top = call(
        functools.partial(attend_kernel, 0),
        "attend_own",
        (jax.ShapeDtypeStruct(acc_shape, F32), jax.ShapeDtypeStruct(top_shape, F32)),
        [SMEM, VMEM, VMEM],
        scratch=[turned_values],
        out_specs=(VMEM, VMEM),
        flops=4 << 30,
    )(pairs, gathered, kv)
    parts = call(
        functools.partial(attend_kernel, 1),
        "attend_other",
        jax.ShapeDtypeStruct(acc_shape, BF16),
        [SMEM] + [VMEM] * 4,
        scratch=[turned_values, pltpu.VMEM(acc_shape, F32), pltpu.VMEM(top_shape, F32)],
        flops=4 << 30,
    )(pairs, gathered, kv_other, acc, top)

    parts = lax.all_to_all(parts, Q_AXES, split_axis=0, concat_axis=0, tiled=True)
    return call(
        merge_kernel, "merge", jax.ShapeDtypeStruct((ROWS, H * DH), F32), [VMEM]
    )(parts)


def solution(mesh):
    fine = Mesh(mesh.devices.reshape(SIZES), AXES)
    by_query = P(AXES, None)
    by_key = P(("zh", "x", "core", "zl", "yh", "yl"), None)
    return jax.shard_map(
        shards,
        mesh=fine,
        in_specs=(by_query, by_key, by_key, P()),
        out_specs=by_query,
        check_vma=False,
    )
```

```python
import functools
import math

import jax
import jax.numpy as jnp
from jax import lax
from jax.experimental import pallas as pl
from jax.experimental.pallas import tpu as pltpu
from jax.sharding import Mesh
from jax.sharding import PartitionSpec as P

H = 4
DH = 128
BLOCK = 128
ROWS = 64
COLS = H * ROWS
NEG_FILL = -1e30
EXP2_SCALE = math.log2(math.e) / math.sqrt(DH)

AXES = ("zl", "yh", "yl", "zh", "x", "core")
SIZES = (2, 4, 2, 4, 4, 2)
Q_AXES = ("zl", "x")
KV_AXES = ("zh", "yh", "yl")
N_OWN = 8
N_KB = 16
N_PAIR = N_OWN * N_KB
LIST = N_PAIR + 8
WIDTHS = (14, 7, 3, 1)
DIAGONAL_WIDTHS = (8, 1)
EXT = DH + 8

F32 = jnp.float32
BF16 = jnp.bfloat16


def plan_kernel(table_ref, pairs_ref):
    yh, yl = lax.axis_index("yh"), lax.axis_index("yl")
    zh, x, zl = lax.axis_index("zh"), lax.axis_index("x"), lax.axis_index("zl")
    core = lax.axis_index("core")
    q_base = (yh * 2 + yl) * 16 + zh * 4
    for side in range(2):
        k_base = x * 16 + (core if side == 0 else 1 - core) * 8 + zl * 4
        full, diag = jnp.int32(0), jnp.int32(0)
        for i in range(N_PAIR):
            kb, own = i // N_OWN, i % N_OWN
            key_block = k_base + (kb // 4) * 64 + kb % 4
            query_block = q_base + (own // 4) * 128 + own % 4
            listed = table_ref[own, key_block]
            on_diag = jnp.where(key_block == query_block, listed, 0)
            pairs_ref[side, 2 + full] = jnp.int32(i)
            pairs_ref[side, LIST - 1 - diag] = jnp.int32(i)
            full = full + (listed - on_diag)
            diag = diag + on_diag
        pairs_ref[side, 0] = full
        pairs_ref[side, 1] = diag


def turn_kernel(rows_ref, out_ref):
    heads = [rows_ref[:, h * DH : (h + 1) * DH] for h in range(H)]
    out_ref[...] = jnp.concatenate(heads, axis=0).T


def split3(x):
    hi = x.astype(BF16)
    rest = x - hi.astype(F32)
    mid = rest.astype(BF16)
    low = (rest - mid.astype(F32)).astype(BF16)
    return hi, mid, low


def attend_kernel(side, pairs_ref, q_ref, kv_ref, *refs):
    if side == 0:
        acc_ref, top_ref, vt_ref = refs
    else:
        acc_before_ref, top_before_ref, out_ref, vt_ref, acc_ref, top_ref = refs
    ones = jnp.ones((EXT - DH, BLOCK), BF16)
    for b in range(N_KB):
        vt_ref[b, :DH, :] = kv_ref[b, :, DH:].T
        vt_ref[b, DH:, :] = ones
    if side == 0:
        acc_ref[...] = jnp.zeros_like(acc_ref)
        top_ref[...] = jnp.full_like(top_ref, NEG_FILL)
    else:
        acc_ref[...] = acc_before_ref[...]
        top_ref[...] = top_before_ref[...]

    def units(entries, diagonal):
        work = [(entry // N_OWN, entry % N_OWN) for entry in entries]
        scores = [
            jnp.dot(kv_ref[kb, :, :DH], q_ref[own], preferred_element_type=F32)
            for kb, own in work
        ]
        if diagonal:
            first = lax.axis_index("core") * ROWS
            key_at = lax.broadcasted_iota(jnp.int32, (BLOCK, COLS), 0)
            row_at = lax.broadcasted_iota(jnp.int32, (BLOCK, COLS), 1) % ROWS
            scores = [jnp.where(key_at <= row_at + first, s, NEG_FILL) for s in scores]
        tops = [jnp.max(s, axis=0, keepdims=True) for s in scores]
        weights = [
            jnp.exp2((s - t) * EXP2_SCALE).astype(BF16) for s, t in zip(scores, tops)
        ]
        parts = [
            jnp.dot(vt_ref[kb], w, preferred_element_type=F32)
            for w, (kb, _) in zip(weights, work)
        ]
        for part, top, (_, own) in zip(parts, tops, work):
            before = top_ref[own]
            after = jnp.maximum(before, top)
            keep = jnp.exp2((before - after) * EXP2_SCALE)
            take = jnp.exp2((top - after) * EXP2_SCALE)
            acc_ref[own] = acc_ref[own] * keep + part * take
            top_ref[own] = after

    full, diag = pairs_ref[side, 0], pairs_ref[side, 1]

    def run(count, widths, entry_at, diagonal):
        done = jnp.int32(0)
        for width in widths:

            def several(i, start, width=width):
                units([entry_at(start + k) for k in range(width)], diagonal)
                return start + width

            done = lax.fori_loop(0, (count - done) // width, several, done)

    run(full, WIDTHS, lambda at: pairs_ref[side, 2 + at], False)
    run(diag, DIAGONAL_WIDTHS, lambda at: pairs_ref[side, LIST - 1 - at], True)
    if side == 0:
        return

    for own in range(N_OWN):
        acc = acc_ref[own]
        out_ref[own, :DH, :] = acc[:DH].astype(BF16)
        fill = jnp.zeros((EXT - DH - 6, COLS), BF16)
        pieces = (*split3(acc[DH : DH + 1]), *split3(top_ref[own]), fill)
        out_ref[own, DH:, :] = jnp.concatenate(pieces, axis=0)


def merge_kernel(parts_ref, out_ref):
    def stat(own, at):
        pieces = parts_ref[own, DH:, :].astype(F32)
        return pieces[at : at + 1] + pieces[at + 1 : at + 2] + pieces[at + 2 : at + 3]

    tops = [stat(own, 3) for own in range(N_OWN)]
    highest = functools.reduce(jnp.maximum, tops)
    factors = [jnp.exp2((t - highest) * EXP2_SCALE) for t in tops]
    total = sum(f * stat(own, 0) for own, f in enumerate(factors))
    mixed = sum(f * parts_ref[own, :DH, :].astype(F32) for own, f in enumerate(factors))
    turned = (mixed / total).T
    for h in range(H):
        out_ref[:, h * DH : (h + 1) * DH] = turned[h * ROWS : (h + 1) * ROWS, :]


VMEM = pl.BlockSpec(memory_space=pltpu.VMEM)
SMEM = pl.BlockSpec(memory_space=pltpu.SMEM)


def call(kernel, name, out_shape, in_specs, scratch=(), out_specs=VMEM, flops=0):
    return pl.pallas_call(
        kernel,
        out_shape=out_shape,
        in_specs=in_specs,
        out_specs=out_specs,
        scratch_shapes=scratch,
        compiler_params=pltpu.CompilerParams(vmem_limit_bytes=16 << 20),
        cost_estimate=pl.CostEstimate(
            flops=flops, bytes_accessed=4 << 20, transcendentals=flops // 512
        ),
        name=name,
    )


def shards(queries, keys, values, block_mask):
    kv = jnp.concatenate((keys, values), axis=1)
    kv = jnp.broadcast_to(kv[None], (2 * N_KB, ROWS, 2 * DH))
    kv = lax.all_to_all(kv, KV_AXES, split_axis=0, concat_axis=0, tiled=True)
    kv = kv.reshape(N_KB, BLOCK, 2 * DH)

    line = (lax.axis_index("yh") * 2 + lax.axis_index("yl")) * 4 + lax.axis_index("zh")
    table = lax.dynamic_index_in_dim(
        block_mask.reshape(2, 32, 4, 256), line, 1, keepdims=False
    ).reshape(N_OWN, 256)
    pairs = call(
        plan_kernel,
        "plan",
        jax.ShapeDtypeStruct((2, LIST), jnp.int32),
        [SMEM],
        out_specs=SMEM,
    )(table)

    turned = call(
        turn_kernel, "turn", jax.ShapeDtypeStruct((DH, COLS), BF16), [VMEM]
    )(queries)
    gathered = lax.all_gather(turned, "x", axis=0, tiled=True)
    gathered, pairs = lax.optimization_barrier((gathered, pairs))
    gathered = lax.all_gather(gathered, "zl", axis=0, tiled=True)
    gathered = gathered.reshape(N_OWN, DH, COLS)

    kv, gathered, pairs = lax.optimization_barrier((kv, gathered, pairs))
    kv_other = lax.ppermute(kv, "core", [(0, 1), (1, 0)])
    acc_shape, top_shape = (N_OWN, EXT, COLS), (N_OWN, 1, COLS)
    turned_values = pltpu.VMEM((N_KB, EXT, BLOCK), BF16)
    acc, top = call(
        functools.partial(attend_kernel, 0),
        "attend_own",
        (jax.ShapeDtypeStruct(acc_shape, F32), jax.ShapeDtypeStruct(top_shape, F32)),
        [SMEM, VMEM, VMEM],
        scratch=[turned_values],
        out_specs=(VMEM, VMEM),
        flops=4 << 30,
    )(pairs, gathered, kv)
    parts = call(
        functools.partial(attend_kernel, 1),
        "attend_other",
        jax.ShapeDtypeStruct(acc_shape, BF16),
        [SMEM] + [VMEM] * 4,
        scratch=[turned_values, pltpu.VMEM(acc_shape, F32), pltpu.VMEM(top_shape, F32)],
        flops=4 << 30,
    )(pairs, gathered, kv_other, acc, top)

    parts = lax.all_to_all(parts, Q_AXES, split_axis=0, concat_axis=0, tiled=True)
    return call(
        merge_kernel, "merge", jax.ShapeDtypeStruct((ROWS, H * DH), F32), [VMEM]
    )(parts)


def solution(mesh):
    fine = Mesh(mesh.devices.reshape(SIZES), AXES)
    by_query = P(AXES, None)
    by_key = P(("zh", "x", "core", "zl", "yh", "yl"), None)
    return jax.shard_map(
        shards,
        mesh=fine,
        in_specs=(by_query, by_key, by_key, P()),
        out_specs=by_query,
        check_vma=False,
    )
```
